512 devices in a mesh: row: 16 (over z_lo, x, core), col: 32 (over y, z_hi).
Axes of the slice: x: 4, y: 8, z: 8 (z_hi: 4, z_lo: 2; z = z_hi * 2 + z_lo), core: 2. Of those that a mesh axis runs over, the one named last changes fastest.
Arguments:
- amplitudes: bfloat16 [1, 8, 4096, 4096], P(None, None, 'row', 'col'), may hold values from -6 to 6
- factors: bfloat16 [1024, 8, 4096], P('col', None, 'row'), may hold values from -0.03125 to 0.03125
Outputs:
- residual: bfloat16 [1, 8, 4096, 4096], P(None, None, 'row', 'col')
The draws below stay inside these ranges and needn't reach their ends.
All inputs are finite; a program needn't handle non-finite values.
Results may differ from the reference program's by a relative error of at most 0.0049.
Values may be sent and summed in bfloat16 or wider, within the bound.
No kernel may reach another device: no remote copies, remote signals or barrier semaphores. Data moves between devices by JAX's collectives and lax.ppermute only.
A program may use at most 64 MiB of HBM per device.

```python
import jax
import jax.numpy as jnp
from jax import lax

V = 4096
AUX = 1024
NI = 1
NJ = 8


def steps_of(key, dims, shards, smallest, top_value):
    factor_of = 1.0
    for position, shards_of in shards:
        heights = jax.random.uniform(jax.random.fold_in(jax.random.fold_in(key, 6), position), (shards_of,), jnp.float32, smallest / len(shards), top_value / len(shards))
        factor_of = factor_of * jnp.repeat(jnp.exp(heights), dims[position] // shards_of).reshape((-1,) + (1,) * (len(dims) - 1 - position))
    return factor_of


def scatter_about(stream_key, extent, deviation, most, pieces=(), kind=jnp.bfloat16):
    entries = jax.random.normal(stream_key, extent, jnp.float32) * deviation
    if len(pieces) > 0:
        entries = steps_of(stream_key, extent, pieces, -0.22, 0.18) * entries
    return jnp.clip(entries, min=-most, max=most).astype(kind)


def setup_inputs(seed: int = 0) -> dict:
    key_list = jax.random.split(jax.random.key(seed), 3)
    return {
        "amplitudes": scatter_about(key_list[0], (NI, NJ, V, V), 1.0, 6.0, ((2, 16), (3, 32))),
        "factors": scatter_about(key_list[1], (AUX, NJ, V), (V * NJ) ** -0.5, 0.03125, ((0, 32), (2, 16))),
    }


def reference(amplitudes, factors):
    by_occupied = jnp.transpose(factors, (1, 0, 2))

    def per_pair(totals, inputs):
        direct, mirror = totals
        slab, factor_slab = inputs
        direct = direct + jnp.dot(factor_slab, slab.T, preferred_element_type=jnp.float32)
        mirror = mirror + jnp.dot(factor_slab, slab, preferred_element_type=jnp.float32)
        return (direct, mirror), None

    def per_occupied(amplitude_rows):
        start = jnp.zeros((factors.shape[0], factors.shape[2]), jnp.float32)
        (direct, mirror), unused = lax.scan(per_pair, (start, start), (amplitude_rows, by_occupied))
        fitted = (2.0 * direct - mirror).astype(jnp.bfloat16)

        def project(factor_slab):
            return jnp.dot(fitted.T, factor_slab, preferred_element_type=jnp.float32).astype(jnp.bfloat16)

        return lax.map(project, by_occupied)

    return lax.map(per_occupied, amplitudes)
```

```python
import jax
import jax.numpy as jnp
from jax import lax
from jax.sharding import PartitionSpec as P

F32 = jnp.float32
BF16 = jnp.bfloat16


def body(amplitudes, factors):
    rows = lax.axis_size("row")
    cols = lax.axis_size("col")
    col_index = lax.axis_index("col")
    _, nj, block_a, block_b = amplitudes.shape
    block_q = factors.shape[0]
    aux = block_q * cols
    t = amplitudes[0]
    odd = lax.rem(col_index, 2)

    by_j = jnp.transpose(factors, (1, 0, 2))
    first, second = by_j[:, :, :block_b], by_j[:, :, block_b:]
    got = []
    for flip in range(2):
        piece = jnp.where(odd == flip, first, second)
        pairs = [
            (r * cols + c, (c // 2) * cols + 2 * r + ((c % 2) ^ flip))
            for r in range(rows)
            for c in range(cols)
        ]
        got.append(lax.ppermute(piece, ("row", "col"), pairs))
    low = jnp.where(odd == 0, got[0], got[1])
    high = jnp.where(odd == 0, got[1], got[0])
    own = jnp.concatenate([low, high], axis=1)

    half = block_b // 2
    x = t.reshape(nj, 2, 2, half, block_b)
    x = jnp.transpose(x, (0, 2, 1, 3, 4)).reshape(rows, 2 * half, block_b)
    x = lax.all_to_all(x, "row", 0, 0, tiled=True)
    x = x.reshape(cols, half, block_b)
    x = lax.all_to_all(x, "col", 0, 0, tiled=True)
    x = x.reshape(rows, 2 * half, block_b)
    x = lax.all_to_all(x, "row", 0, 0, tiled=True)
    x = x.reshape(nj, 2, 2, half, block_b)
    swapped = jnp.transpose(x, (0, 1, 3, 2, 4)).reshape(nj, block_b, block_a)

    gathered = lax.all_gather(own, "row", axis=1, tiled=True)

    direct = jnp.einsum("jab,jqb->qa", t, gathered, preferred_element_type=F32)
    mirror = jnp.einsum("jqs,jsa->qa", gathered, swapped, preferred_element_type=F32)
    partial = (2.0 * direct - mirror).astype(BF16)

    parts = partial.reshape(cols, block_q, block_a)
    parts = lax.all_to_all(parts, "col", 0, 0, tiled=True)
    shard = jnp.sum(parts.astype(F32), axis=0).astype(BF16)
    copies = jnp.broadcast_to(shard[None], (cols, block_q, block_a))
    fitted = lax.all_to_all(copies, "col", 0, 0, tiled=True).reshape(aux, block_a)

    result = jnp.einsum("qa,jqb->jab", fitted, gathered, preferred_element_type=F32)
    return result.astype(BF16)[None]


def solution(mesh):
    placed = (P(None, None, "row", "col"), P("col", None, "row"))
    return jax.shard_map(
        body, mesh=mesh, in_specs=placed, out_specs=P(None, None, "row", "col"), check_vma=False
    )
```

```python
import jax
import jax.numpy as jnp
from jax import lax
from jax.sharding import Mesh, PartitionSpec as P

F32 = jnp.float32
BF16 = jnp.bfloat16


def exchange(value, axes):
    return lax.all_to_all(value, axes, 0, 0, tiled=True)


def body(amplitudes, factors):
    cores = lax.axis_size("core")
    chips = lax.axis_size("chip")
    cols = lax.axis_size("col")
    rows = chips * cores
    _, nj, block_a, block_b = amplitudes.shape
    block_q = factors.shape[0]
    aux = block_q * cols
    half = block_b // 2
    few = block_q // 2
    t = amplitudes[0]

    x = jnp.transpose(t.reshape(nj, 2, 2, half, block_b), (0, 2, 1, 3, 4))
    x = x.reshape(rows, 2, half, block_b)
    y = jnp.transpose(factors.reshape(2, few, nj, 2, block_b), (2, 0, 3, 1, 4))
    y = y.reshape(rows, 2, few, block_b)
    both = jnp.concatenate([x, y], axis=2)
    both = exchange(both, ("chip", "core"))
    both = both.reshape(cols, half + few, block_b)
    both = exchange(both, "col")
    x, y = both[:, :half], both[:, half:]

    x = x.reshape(chips, 2 * 2 * half, block_b)
    y = jnp.broadcast_to(y.reshape(1, cols * few, block_b), (chips, cols * few, block_b))
    both = exchange(jnp.concatenate([x, y], axis=1), "chip")
    x, own = both[:, : 4 * half], both[:, 4 * half :]

    other = lax.ppermute(own, "core", [(k, (k + 1) % 2) for k in range(2)])
    x = jnp.transpose(x.reshape(nj, 2, 2, half, block_b), (1, 0, 2, 3, 4))
    x = exchange(x.reshape(2, nj * 2 * half, block_b), "core")
    x = x.reshape(2, nj, 2, half, block_b)
    swapped = jnp.transpose(x, (1, 0, 3, 2, 4)).reshape(nj, block_b, block_a)

    pieces = []
    for held in (own, other):
        direct = jnp.einsum("jab,jqb->qa", t, held, preferred_element_type=F32)
        mirror = jnp.einsum("jqs,jsa->qa", held, swapped, preferred_element_type=F32)
        pieces.append((2.0 * direct - mirror).astype(BF16))
    parts = jnp.concatenate(pieces, axis=0).reshape(cols, block_q, block_a)

    parts = exchange(parts, "col")
    shard = jnp.sum(parts.astype(F32), axis=0).astype(BF16)
    copies = jnp.broadcast_to(shard[None], (cols, block_q, block_a))
    fitted = exchange(copies, "col").reshape(2, aux // 2, block_a)

    result = jnp.einsum("qa,jqb->jab", fitted[0], own, preferred_element_type=F32)
    result = result + jnp.einsum("qa,jqb->jab", fitted[1], other, preferred_element_type=F32)
    return result.astype(BF16)[None]


def solution(mesh):
    rows, cols = mesh.devices.shape
    fine = Mesh(mesh.devices.reshape(rows // 2, 2, cols), ("chip", "core", "col"))
    row = ("chip", "core")
    placed = (P(None, None, row, "col"), P("col", None, row))
    return jax.shard_map(
        body, mesh=fine, in_specs=placed, out_specs=P(None, None, row, "col"), check_vma=False
    )
```

```python
import jax
import jax.numpy as jnp
from jax import lax
from jax.sharding import Mesh, PartitionSpec as P

F32 = jnp.float32
BF16 = jnp.bfloat16
ROW = ("chip", "core")


def exchange(value, axes):
    return lax.all_to_all(value, axes, 0, 0, tiled=True)


def body(amplitudes, factors):
    cores = lax.axis_size("core")
    chips = lax.axis_size("chip")
    cols = lax.axis_size("col")
    rows = chips * cores
    _, nj, block_a, block_b = amplitudes.shape
    block_q = factors.shape[0]
    half = block_b // 2
    odd = lax.rem(lax.axis_index("col"), 2)
    t = amplitudes[0]

    by_j = jnp.transpose(factors, (1, 0, 2))
    first, second = by_j[:, :, :block_b], by_j[:, :, block_b:]
    got = []
    for flip in range(2):
        pairs = [
            (r * cols + c, (c // 2) * cols + 2 * r + ((c % 2) ^ flip))
            for r in range(rows)
            for c in range(cols)
        ]
        got.append(lax.ppermute(jnp.where(odd == flip, first, second), ROW + ("col",), pairs))
    low = jnp.where(odd == 0, got[0], got[1])
    high = jnp.where(odd == 0, got[1], got[0])
    own = jnp.concatenate([low, high], axis=1)

    x = jnp.transpose(t.reshape(nj, 2, 2, half, block_b), (0, 2, 1, 3, 4))
    x = exchange(x.reshape(rows, 2 * half, block_b), ROW)

    held = [own]
    for step in range(1, chips):
        held.append(lax.ppermute(own, "chip", [(i, i ^ step) for i in range(chips)]))
    mine = jnp.stack(held)
    theirs = lax.ppermute(mine, "core", [(0, 1), (1, 0)])

    x = exchange(x.reshape(cols, half, block_b), "col")
    x = exchange(x.reshape(rows, 2 * half, block_b), ROW)
    x = x.reshape(nj, 2, 2, half, block_b)
    swapped = jnp.transpose(x, (0, 1, 3, 2, 4)).reshape(nj, block_b, block_a)

    pieces = []
    for part in (mine, theirs):
        direct = jnp.einsum("jab,sjqb->sqa", t, part, preferred_element_type=F32)
        mirror = jnp.einsum("sjqv,jva->sqa", part, swapped, preferred_element_type=F32)
        pieces.append((2.0 * direct - mirror).astype(BF16))
    parts = jnp.concatenate(pieces, axis=0).reshape(cols, block_q, block_a)

    parts = exchange(parts, "col")
    shard = jnp.sum(parts.astype(F32), axis=0).astype(BF16)
    copies = jnp.broadcast_to(shard[None], (cols, block_q, block_a))
    fitted = exchange(copies, "col").reshape(2, chips, 2 * block_q, block_a)

    result = jnp.einsum("sqa,sjqb->jab", fitted[0], mine, preferred_element_type=F32)
    result = result + jnp.einsum("sqa,sjqb->jab", fitted[1], theirs, preferred_element_type=F32)
    return result.astype(BF16)[None]


def solution(mesh):
    rows, cols = mesh.devices.shape
    fine = Mesh(mesh.devices.reshape(rows // 2, 2, cols), ("chip", "core", "col"))
    placed = (P(None, None, ROW, "col"), P("col", None, ROW))
    return jax.shard_map(
        body, mesh=fine, in_specs=placed, out_specs=P(None, None, ROW, "col"), check_vma=False
    )
```

```python
import jax
import jax.numpy as jnp
from jax import lax
from jax.sharding import Mesh, PartitionSpec as P

F32 = jnp.float32
BF16 = jnp.bfloat16
ROW = ("chip", "core")
SWAP = [(0, 1), (1, 0)]


def exchange(value, axes):
    return lax.all_to_all(value, axes, 0, 0, tiled=True)


def in_core_order(core, mine, theirs):
    first = jnp.where(core == 0, mine, theirs)
    second = jnp.where(core == 0, theirs, mine)
    return first, second


def body(amplitudes, factors):
    core = lax.axis_index("core")
    chips = lax.axis_size("chip")
    cols = lax.axis_size("col")
    _, nj, block_a, block_b = amplitudes.shape
    block_q = factors.shape[0]
    aux = block_q * cols
    half = block_b // 2
    few = block_q // 2
    per_core = nj // 2
    t = amplitudes[0].reshape(2, per_core, block_a, block_b)

    x = jnp.transpose(t.reshape(2, per_core, 2, 2, half, block_b), (1, 3, 0, 2, 4, 5))
    x = x.reshape(chips * 2, 2, half, block_b)
    y = jnp.transpose(factors.reshape(2, few, 2, per_core, 2, block_b), (3, 0, 2, 4, 1, 5))
    y = y.reshape(chips * 2, 2, few, block_b)
    both = exchange(jnp.concatenate([x, y], axis=2), ROW)
    both = exchange(both.reshape(cols, half + few, block_b), "col")
    x, y = both[:, :half], both[:, half:]

    sent = jnp.where(core == 0, t[1], t[0])
    kept = jnp.where(core == 0, t[0], t[1])
    straight = in_core_order(core, kept, lax.ppermute(sent, "core", SWAP))

    x = x.reshape(chips, 4 * half, block_b)
    y = jnp.broadcast_to(y.reshape(1, cols * few, block_b), (chips, cols * few, block_b))
    both = exchange(jnp.concatenate([x, y], axis=1), "chip")
    mine = both[:, 4 * half :].reshape(per_core, aux, block_b)
    x = both[:, : 4 * half].reshape(per_core, 2, 2, 2, half, block_b)
    swapped = jnp.transpose(x, (2, 0, 1, 4, 3, 5)).reshape(2, per_core, block_b, block_a)

    pieces = []
    for h in range(2):
        direct = jnp.einsum("jab,jqb->qa", straight[h], mine, preferred_element_type=F32)
        mirror = jnp.einsum("jqv,jva->qa", mine, swapped[h], preferred_element_type=F32)
        pieces.append((2.0 * direct - mirror).astype(BF16))
    pieces = exchange(jnp.stack(pieces), "core")
    partial = (pieces[0].astype(F32) + pieces[1].astype(F32)).astype(BF16)

    theirs = lax.ppermute(mine, "core", SWAP)
    low, high = in_core_order(core, mine, theirs)

    parts = exchange(partial.reshape(cols, block_q, block_a), "col")
    shard = jnp.sum(parts.astype(F32), axis=0).astype(BF16)
    copies = jnp.broadcast_to(shard[None], (cols, block_q, block_a))
    fitted = exchange(copies, "col").reshape(aux, block_a)

    held = jnp.concatenate([low, high], axis=0)
    result = jnp.einsum("qa,jqb->jab", fitted, held, preferred_element_type=F32)
    return result.astype(BF16)[None]


def solution(mesh):
    rows, cols = mesh.devices.shape
    fine = Mesh(mesh.devices.reshape(rows // 2, 2, cols), ("chip", "core", "col"))
    placed = (P(None, None, ROW, "col"), P("col", None, ROW))
    return jax.shard_map(
        body, mesh=fine, in_specs=placed, out_specs=P(None, None, ROW, "col"), check_vma=False
    )
```

```python
import jax
import jax.numpy as jnp
from jax import lax
from jax.experimental import pallas as pl
from jax.experimental.pallas import tpu as pltpu
from jax.sharding import Mesh, PartitionSpec as P

F32 = jnp.float32
BF16 = jnp.bfloat16
ROW = ("chip", "core")
VMEM = pl.BlockSpec(memory_space=pltpu.VMEM)


def exchange(value, axes):
    return lax.all_to_all(value, axes, 0, 0, tiled=True)


def fit_kernel(both_ref, t_ref, out_ref):
    nj, block_a, block_b = t_ref.shape
    half = block_b // 2
    aux_half = both_ref.shape[2] - block_b
    straight = jnp.concatenate([t_ref[j] for j in range(nj)], axis=1)
    columns = []
    for side in range(2):
        rows = pl.ds(side * half, half)
        columns.append(
            jnp.concatenate([both_ref[s, j, rows, :] for j in range(nj) for s in range(2)], axis=0)
        )
    swapped = jnp.concatenate(columns, axis=1)
    for s in range(2):
        held = jnp.concatenate(
            [both_ref[s, j, pl.ds(block_b, aux_half), :] for j in range(nj)], axis=1
        )
        direct = lax.dot_general(
            held, straight, (((1,), (1,)), ((), ())), preferred_element_type=F32
        )
        mirror = jnp.dot(held, swapped, preferred_element_type=F32)
        out_ref[pl.ds(s * aux_half, aux_half), :] = (2.0 * direct - mirror).astype(BF16)


def body(amplitudes, factors):
    cores = lax.axis_size("core")
    chips = lax.axis_size("chip")
    cols = lax.axis_size("col")
    rows = chips * cores
    _, nj, block_a, block_b = amplitudes.shape
    block_q = factors.shape[0]
    aux = block_q * cols
    half = block_b // 2
    few = block_q // 2
    t = amplitudes[0]

    x = jnp.transpose(t.reshape(nj, 2, 2, half, block_b), (0, 2, 1, 3, 4))
    x = x.reshape(rows, 2, half, block_b)
    y = jnp.transpose(factors.reshape(2, few, nj, 2, block_b), (2, 0, 3, 1, 4))
    y = y.reshape(rows, 2, few, block_b)
    both = exchange(jnp.concatenate([x, y], axis=2), ROW)
    both = exchange(both.reshape(cols, half + few, block_b), "col")
    x, y = both[:, :half], both[:, half:]

    x = x.reshape(chips, 4 * half, block_b)
    y = jnp.broadcast_to(y.reshape(1, cols * few, block_b), (chips, cols * few, block_b))
    both = exchange(jnp.concatenate([x, y], axis=1), "chip")

    x = jnp.transpose(both[:, : 4 * half].reshape(nj, 2, block_b, block_b), (1, 0, 2, 3))
    y = jnp.broadcast_to(both[None, :, 4 * half :], (2, nj, aux // 2, block_b))
    both = exchange(jnp.concatenate([x, y], axis=2), "core")

    partial = pl.pallas_call(
        fit_kernel,
        out_shape=jax.ShapeDtypeStruct((aux, block_a), BF16),
        in_specs=[VMEM, VMEM],
        out_specs=VMEM,
        compiler_params=pltpu.CompilerParams(vmem_limit_bytes=32 << 20),
        cost_estimate=pl.CostEstimate(
            flops=4 * aux * block_a * nj * block_b, bytes_accessed=4 << 20, transcendentals=0
        ),
    )(both, t)

    parts = exchange(partial.reshape(cols, block_q, block_a), "col")
    shard = jnp.sum(parts.astype(F32), axis=0).astype(BF16)
    copies = jnp.broadcast_to(shard[None], (cols, block_q, block_a))
    fitted = exchange(copies, "col").reshape(2, aux // 2, block_a)

    held = both[:, :, block_b:]
    result = jnp.einsum("sqa,sjqb->jab", fitted, held, preferred_element_type=F32)
    return result.astype(BF16)[None]


def solution(mesh):
    rows, cols = mesh.devices.shape
    fine = Mesh(mesh.devices.reshape(rows // 2, 2, cols), ("chip", "core", "col"))
    placed = (P(None, None, ROW, "col"), P("col", None, ROW))
    return jax.shard_map(
        body, mesh=fine, in_specs=placed, out_specs=P(None, None, ROW, "col"), check_vma=False
    )
```

```python
import jax
import jax.numpy as jnp
from jax import lax
from jax.experimental import pallas as pl
from jax.experimental.pallas import tpu as pltpu
from jax.sharding import Mesh, PartitionSpec as P

F32 = jnp.float32
BF16 = jnp.bfloat16
ROW = ("chip", "core")
VMEM = pl.BlockSpec(memory_space=pltpu.VMEM)


def exchange(value, axes):
    return lax.all_to_all(value, axes, 0, 0, tiled=True)


def fit_kernel(both_ref, t_ref, out_ref):
    nj, block_a, block_b = t_ref.shape
    half = block_b // 2
    aux_half = both_ref.shape[2] - block_b
    straight = jnp.concatenate([t_ref[j] for j in range(nj)], axis=1)
    columns = []
    for side in range(2):
        rows = pl.ds(side * half, half)
        columns.append(
            jnp.concatenate([both_ref[s, j, rows, :] for j in range(nj) for s in range(2)], axis=0)
        )
    swapped = jnp.concatenate(columns, axis=1)
    for s in range(2):
        held = jnp.concatenate(
            [both_ref[s, j, pl.ds(block_b, aux_half), :] for j in range(nj)], axis=1
        )
        direct = lax.dot_general(
            held, straight, (((1,), (1,)), ((), ())), preferred_element_type=F32
        )
        mirror = jnp.dot(held, swapped, preferred_element_type=F32)
        out_ref[pl.ds(s * aux_half, aux_half), :] = (2.0 * direct - mirror).astype(BF16)


def pack_kernel(t_ref, f_ref, out_ref):
    nj, _, block_b = t_ref.shape
    half = block_b // 2
    few = f_ref.shape[0] // 2
    for j in range(nj):
        for bit in range(2):
            for side in range(2):
                rows = pl.ds(side * block_b + bit * half, half)
                out_ref[2 * j + bit, side, pl.ds(0, half), :] = t_ref[j, rows, :]
    for bit in range(2):
        for side in range(2):
            piece = f_ref[pl.ds(bit * few, few), :, pl.ds(side * block_b, block_b)]
            by_j = jnp.swapaxes(piece.astype(F32), 0, 1).astype(BF16)
            for j in range(nj):
                out_ref[2 * j + bit, side, pl.ds(half, few), :] = by_j[j]


def project_kernel(fitted_ref, both_ref, out_ref):
    nj, _, block_b = out_ref.shape
    aux_half = fitted_ref.shape[0] // 2
    total = None
    for s in range(2):
        held = jnp.concatenate(
            [both_ref[s, j, pl.ds(block_b, aux_half), :] for j in range(nj)], axis=1
        )
        term = lax.dot_general(
            fitted_ref[pl.ds(s * aux_half, aux_half), :],
            held,
            (((0,), (0,)), ((), ())),
            preferred_element_type=F32,
        )
        total = term if total is None else total + term
    for j in range(nj):
        out_ref[j] = total[:, j * block_b : (j + 1) * block_b].astype(BF16)


def call(kernel, shape, *operands):
    return pl.pallas_call(
        kernel,
        out_shape=jax.ShapeDtypeStruct(shape, BF16),
        in_specs=[VMEM] * len(operands),
        out_specs=VMEM,
        compiler_params=pltpu.CompilerParams(vmem_limit_bytes=32 << 20),
    )(*operands)


def body(amplitudes, factors):
    cores = lax.axis_size("core")
    chips = lax.axis_size("chip")
    cols = lax.axis_size("col")
    rows = chips * cores
    _, nj, block_a, block_b = amplitudes.shape
    block_q = factors.shape[0]
    aux = block_q * cols
    half = block_b // 2
    few = block_q // 2
    t = amplitudes[0]

    both = exchange(call(pack_kernel, (rows, 2, half + few, block_b), t, factors), ROW)
    both = exchange(both.reshape(cols, half + few, block_b), "col")
    x, y = both[:, :half], both[:, half:]

    x = x.reshape(chips, 4 * half, block_b)
    y = jnp.broadcast_to(y.reshape(1, cols * few, block_b), (chips, cols * few, block_b))
    both = exchange(jnp.concatenate([x, y], axis=1), "chip")

    x = jnp.transpose(both[:, : 4 * half].reshape(nj, 2, block_b, block_b), (1, 0, 2, 3))
    y = jnp.broadcast_to(both[None, :, 4 * half :], (2, nj, aux // 2, block_b))
    both = exchange(jnp.concatenate([x, y], axis=2), "core")

    partial = call(fit_kernel, (aux, block_a), both, t)

    parts = exchange(partial.reshape(cols, block_q, block_a), "col")
    shard = jnp.sum(parts.astype(F32), axis=0).astype(BF16)
    copies = jnp.broadcast_to(shard[None], (cols, block_q, block_a))
    fitted = exchange(copies, "col").reshape(aux, block_a)

    return call(project_kernel, (nj, block_a, block_b), fitted, both)[None]


def solution(mesh):
    rows, cols = mesh.devices.shape
    fine = Mesh(mesh.devices.reshape(rows // 2, 2, cols), ("chip", "core", "col"))
    placed = (P(None, None, ROW, "col"), P("col", None, ROW))
    return jax.shard_map(
        body, mesh=fine, in_specs=placed, out_specs=P(None, None, ROW, "col"), check_vma=False
    )
```

```python
import jax
import jax.numpy as jnp
from jax import lax
from jax.experimental import pallas as pl
from jax.experimental.pallas import tpu as pltpu
from jax.sharding import Mesh, PartitionSpec as P

F32 = jnp.float32
BF16 = jnp.bfloat16
ROW = ("chip", "core")
VMEM = pl.BlockSpec(memory_space=pltpu.VMEM)
HBM = pl.BlockSpec(memory_space=pltpu.HBM)


def exchange(value, axes):
    return lax.all_to_all(value, axes, 0, 0, tiled=True)


def fit_kernel(both_ref, t_ref, out_ref):
    _, nj, block_a, block_b = t_ref.shape
    half = block_b // 2
    aux_half = both_ref.shape[2] - block_b
    straight = jnp.concatenate([t_ref[0, j] for j in range(nj)], axis=1)
    columns = []
    for side in range(2):
        rows = pl.ds(side * half, half)
        columns.append(
            jnp.concatenate([both_ref[s, j, rows, :] for j in range(nj) for s in range(2)], axis=0)
        )
    swapped = jnp.concatenate(columns, axis=1)
    for s in range(2):
        held = jnp.concatenate(
            [both_ref[s, j, pl.ds(block_b, aux_half), :] for j in range(nj)], axis=1
        )
        direct = lax.dot_general(
            held, straight, (((1,), (1,)), ((), ())), preferred_element_type=F32
        )
        mirror = jnp.dot(held, swapped, preferred_element_type=F32)
        out_ref[pl.ds(s * aux_half, aux_half), :] = (2.0 * direct - mirror).astype(BF16)


def pack_kernel(t_hbm, f_hbm, out_ref, t_ref, f_ref, sems):
    _, nj, _, block_b = t_ref.shape
    half = block_b // 2
    few = f_ref.shape[0] // 2
    load_f = pltpu.make_async_copy(f_hbm, f_ref, sems.at[0])
    load_t = pltpu.make_async_copy(t_hbm, t_ref, sems.at[1])
    load_f.start()
    load_t.start()
    load_f.wait()
    for bit in range(2):
        for side in range(2):
            piece = f_ref[pl.ds(bit * few, few), :, pl.ds(side * block_b, block_b)]
            by_j = jnp.swapaxes(piece.astype(F32), 0, 1).astype(BF16)
            for j in range(nj):
                out_ref[2 * j + bit, side, pl.ds(half, few), :] = by_j[j]
    load_t.wait()
    for bit in range(2):
        for side in range(2):
            rows = pl.ds(side * block_b + bit * half, half)
            for j in range(nj):
                out_ref[2 * j + bit, side, pl.ds(0, half), :] = t_ref[0, j, rows, :]


def project_kernel(fitted_ref, both_ref, out_hbm, out_ref, sems):
    _, nj, _, block_b = out_ref.shape
    aux_half = fitted_ref.shape[0] // 2
    turned = fitted_ref[...].T
    stores = []
    for j in range(0, nj, 2):
        held = jnp.concatenate(
            [
                jnp.concatenate(
                    [both_ref[s, j + i, pl.ds(block_b, aux_half), :] for s in range(2)], axis=0
                )
                for i in range(2)
            ],
            axis=1,
        )
        total = jnp.dot(turned, held, preferred_element_type=F32).astype(BF16)
        for i in range(2):
            out_ref[0, j + i] = total[:, i * block_b : (i + 1) * block_b]
            store = pltpu.make_async_copy(out_ref.at[0, j + i], out_hbm.at[0, j + i], sems.at[j + i])
            store.start()
            stores.append(store)
    for store in stores:
        store.wait()


def call(kernel, shapes, operands, inside=VMEM, outside=VMEM, scratch=()):
    return pl.pallas_call(
        kernel,
        out_shape=[jax.ShapeDtypeStruct(shape, BF16) for shape in shapes],
        in_specs=[inside] * len(operands),
        out_specs=[outside] * len(shapes),
        scratch_shapes=scratch,
        compiler_params=pltpu.CompilerParams(vmem_limit_bytes=32 << 20),
    )(*operands)


def body(amplitudes, factors):
    cores = lax.axis_size("core")
    chips = lax.axis_size("chip")
    cols = lax.axis_size("col")
    rows = chips * cores
    _, nj, block_a, block_b = amplitudes.shape
    block_q = factors.shape[0]
    aux = block_q * cols
    half = block_b // 2
    few = block_q // 2

    both, kept = call(
        pack_kernel,
        [(rows, 2, half + few, block_b), amplitudes.shape],
        [pltpu.with_memory_space_constraint(x, pltpu.HBM) for x in (amplitudes, factors)],
        inside=HBM,
        scratch=[pltpu.VMEM(factors.shape, BF16), pltpu.SemaphoreType.DMA((2,))],
    )
    both = exchange(both, ROW)
    both = exchange(both.reshape(cols, half + few, block_b), "col")
    x, y = both[:, :half], both[:, half:]

    x = x.reshape(chips, 4 * half, block_b)
    y = jnp.broadcast_to(y.reshape(1, cols * few, block_b), (chips, cols * few, block_b))
    both = exchange(jnp.concatenate([x, y], axis=1), "chip")

    x = jnp.transpose(both[:, : 4 * half].reshape(nj, 2, block_b, block_b), (1, 0, 2, 3))
    y = jnp.broadcast_to(both[None, :, 4 * half :], (2, nj, aux // 2, block_b))
    both = exchange(jnp.concatenate([x, y], axis=2), "core")

    (partial,) = call(fit_kernel, [(aux, block_a)], [both, kept])

    parts = exchange(partial.reshape(cols, block_q, block_a), "col")
    shard = jnp.sum(parts.astype(F32), axis=0).astype(BF16)
    copies = jnp.broadcast_to(shard[None], (cols, block_q, block_a))
    fitted = exchange(copies, "col").reshape(aux, block_a)

    (result,) = call(
        project_kernel,
        [amplitudes.shape],
        [fitted, both],
        outside=HBM,
        scratch=[pltpu.VMEM(amplitudes.shape, BF16), pltpu.SemaphoreType.DMA((nj,))],
    )
    return result


def solution(mesh):
    rows, cols = mesh.devices.shape
    fine = Mesh(mesh.devices.reshape(rows // 2, 2, cols), ("chip", "core", "col"))
    placed = (P(None, None, ROW, "col"), P("col", None, ROW))
    return jax.shard_map(
        body, mesh=fine, in_specs=placed, out_specs=P(None, None, ROW, "col"), check_vma=False
    )
```

```python
import jax
import jax.numpy as jnp
from jax import lax
from jax.experimental import pallas as pl
from jax.experimental.pallas import tpu as pltpu
from jax.sharding import Mesh, PartitionSpec as P

F32 = jnp.float32
BF16 = jnp.bfloat16
ROW = ("chip", "core")
VMEM = pl.BlockSpec(memory_space=pltpu.VMEM)
HBM = pl.BlockSpec(memory_space=pltpu.HBM)


def exchange(value, axes):
    return lax.all_to_all(value, axes, 0, 0, tiled=True)


def places(core, block_b, aux_half):
    own_t = pl.multiple_of(core * (block_b + aux_half), block_b)
    other_t = pl.multiple_of(core * aux_half, block_b)
    other_f = pl.multiple_of((1 - core) * block_b, block_b)
    return own_t, other_t, other_f


def fit_kernel(own_ref, other_ref, t_ref, out_ref):
    _, nj, block_a, block_b = t_ref.shape
    half = block_b // 2
    aux_half = out_ref.shape[0] // 2
    core = lax.axis_index("core")
    own_t, other_t, other_f = places(core, block_b, aux_half)
    straight = jnp.concatenate([t_ref[0, j] for j in range(nj)], axis=1)
    columns = []
    for side in range(2):
        blocks = []
        for j in range(nj):
            mine = own_ref[j, pl.ds(own_t + side * half, half), :]
            theirs = other_ref[j, pl.ds(other_t + side * half, half), :]
            blocks.append(jnp.where(core == 0, mine, theirs))
            blocks.append(jnp.where(core == 0, theirs, mine))
        columns.append(jnp.concatenate(blocks, axis=0))
    swapped = jnp.concatenate(columns, axis=1)
    for s, (ref, start) in enumerate(((own_ref, block_b), (other_ref, other_f))):
        held = jnp.concatenate([ref[j, pl.ds(start, aux_half), :] for j in range(nj)], axis=1)
        direct = lax.dot_general(
            held, straight, (((1,), (1,)), ((), ())), preferred_element_type=F32
        )
        mirror = jnp.dot(held, swapped, preferred_element_type=F32)
        out_ref[pl.ds(s * aux_half, aux_half), :] = (2.0 * direct - mirror).astype(BF16)


def pack_kernel(t_hbm, f_hbm, out_ref, t_ref, f_ref, sems):
    _, nj, _, block_b = t_ref.shape
    half = block_b // 2
    few = f_ref.shape[0] // 2
    load_f = pltpu.make_async_copy(f_hbm, f_ref, sems.at[0])
    load_t = pltpu.make_async_copy(t_hbm, t_ref, sems.at[1])
    load_f.start()
    load_t.start()
    load_f.wait()
    for bit in range(2):
        for side in range(2):
            piece = f_ref[pl.ds(bit * few, few), :, pl.ds(side * block_b, block_b)]
            by_j = jnp.swapaxes(piece.astype(F32), 0, 1).astype(BF16)
            for j in range(nj):
                out_ref[2 * j + bit, side, pl.ds(half, few), :] = by_j[j]
    load_t.wait()
    for bit in range(2):
        for side in range(2):
            rows = pl.ds(side * block_b + bit * half, half)
            for j in range(nj):
                out_ref[2 * j + bit, side, pl.ds(0, half), :] = t_ref[0, j, rows, :]


def project_kernel(fitted_ref, own_ref, other_ref, out_hbm, out_ref, sems):
    _, nj, _, block_b = out_ref.shape
    aux_half = fitted_ref.shape[0] // 2
    _, _, other_f = places(lax.axis_index("core"), block_b, aux_half)
    turned = fitted_ref[...].T
    stores = []
    for j in range(0, nj, 2):
        held = jnp.concatenate(
            [
                jnp.concatenate(
                    [
                        own_ref[j + i, pl.ds(block_b, aux_half), :],
                        other_ref[j + i, pl.ds(other_f, aux_half), :],
                    ],
                    axis=0,
                )
                for i in range(2)
            ],
            axis=1,
        )
        total = jnp.dot(turned, held, preferred_element_type=F32).astype(BF16)
        for i in range(2):
            out_ref[0, j + i] = total[:, i * block_b : (i + 1) * block_b]
            store = pltpu.make_async_copy(out_ref.at[0, j + i], out_hbm.at[0, j + i], sems.at[j + i])
            store.start()
            stores.append(store)
    for store in stores:
        store.wait()


def call(kernel, shapes, operands, inside=VMEM, outside=VMEM, scratch=()):
    return pl.pallas_call(
        kernel,
        out_shape=[jax.ShapeDtypeStruct(shape, BF16) for shape in shapes],
        in_specs=[inside] * len(operands),
        out_specs=[outside] * len(shapes),
        scratch_shapes=scratch,
        compiler_params=pltpu.CompilerParams(vmem_limit_bytes=32 << 20),
    )(*operands)


def body(amplitudes, factors):
    cores = lax.axis_size("core")
    chips = lax.axis_size("chip")
    cols = lax.axis_size("col")
    rows = chips * cores
    _, nj, block_a, block_b = amplitudes.shape
    block_q = factors.shape[0]
    aux = block_q * cols
    half = block_b // 2
    few = block_q // 2

    both, kept = call(
        pack_kernel,
        [(rows, 2, half + few, block_b), amplitudes.shape],
        [pltpu.with_memory_space_constraint(x, pltpu.HBM) for x in (amplitudes, factors)],
        inside=HBM,
        scratch=[pltpu.VMEM(factors.shape, BF16), pltpu.SemaphoreType.DMA((2,))],
    )
    start = ((1 - lax.axis_index("core")) * block_b).astype(jnp.uint32)
    both, start = lax.optimization_barrier((both, start))
    both = exchange(both, ROW)
    both = exchange(both.reshape(cols, half + few, block_b), "col")
    x, y = both[:, :half], both[:, half:]

    x = x.reshape(chips, 2, block_b, block_b)
    y = jnp.broadcast_to(y.reshape(1, cols * few, block_b), (chips, cols * few, block_b))
    own = exchange(jnp.concatenate([x[:, 0], y, x[:, 1]], axis=1), "chip")

    zero = jnp.uint32(0)
    other = lax.dynamic_slice(own, (zero, start, zero), (chips, block_b + aux // 2, block_b))
    other = lax.ppermute(other, "core", [(0, 1), (1, 0)])

    (partial,) = call(fit_kernel, [(aux, block_a)], [own, other, kept])

    parts = exchange(partial.reshape(cols, block_q, block_a), "col")
    shard = jnp.sum(parts.astype(F32), axis=0).astype(BF16)
    copies = jnp.broadcast_to(shard[None], (cols, block_q, block_a))
    fitted = exchange(copies, "col").reshape(aux, block_a)

    (result,) = call(
        project_kernel,
        [amplitudes.shape],
        [fitted, own, other],
        outside=HBM,
        scratch=[pltpu.VMEM(amplitudes.shape, BF16), pltpu.SemaphoreType.DMA((nj,))],
    )
    return result


def solution(mesh):
    rows, cols = mesh.devices.shape
    fine = Mesh(mesh.devices.reshape(rows // 2, 2, cols), ("chip", "core", "col"))
    placed = (P(None, None, ROW, "col"), P("col", None, ROW))
    return jax.shard_map(
        body, mesh=fine, in_specs=placed, out_specs=P(None, None, ROW, "col"), check_vma=False
    )
```

```python
import jax
import jax.numpy as jnp
from jax import lax
from jax.experimental import pallas as pl
from jax.experimental.pallas import tpu as pltpu
from jax.sharding import Mesh, PartitionSpec as P

F32 = jnp.float32
BF16 = jnp.bfloat16
ROW = ("chip", "core")
VMEM = pl.BlockSpec(memory_space=pltpu.VMEM)
HBM = pl.BlockSpec(memory_space=pltpu.HBM)


def exchange(value, axes):
    return lax.all_to_all(value, axes, 0, 0, tiled=True)


def places(core, block_b, aux_half):
    own_t = pl.multiple_of(core * (block_b + aux_half), block_b)
    other_t = pl.multiple_of(core * aux_half, block_b)
    other_f = pl.multiple_of((1 - core) * block_b, block_b)
    return own_t, other_t, other_f


def early_kernel(own_ref, t_ref, out_ref):
    _, nj, _, block_b = t_ref.shape
    aux_half = out_ref.shape[0]
    held = jnp.concatenate([own_ref[j, pl.ds(block_b, aux_half), :] for j in range(nj)], axis=1)
    straight = jnp.concatenate([t_ref[0, j] for j in range(nj)], axis=1)
    out_ref[...] = 2.0 * lax.dot_general(
        held, straight, (((1,), (1,)), ((), ())), preferred_element_type=F32
    )


def fit_kernel(own_ref, other_ref, t_ref, early_ref, out_ref):
    _, nj, block_a, block_b = t_ref.shape
    half = block_b // 2
    aux_half = out_ref.shape[0] // 2
    core = lax.axis_index("core")
    own_t, other_t, other_f = places(core, block_b, aux_half)
    columns = []
    for side in range(2):
        blocks = []
        for j in range(nj):
            mine = own_ref[j, pl.ds(own_t + side * half, half), :]
            theirs = other_ref[j, pl.ds(other_t + side * half, half), :]
            blocks.append(jnp.where(core == 0, mine, theirs))
            blocks.append(jnp.where(core == 0, theirs, mine))
        columns.append(jnp.concatenate(blocks, axis=0))
    swapped = jnp.concatenate(columns, axis=1)
    held = jnp.concatenate([own_ref[j, pl.ds(block_b, aux_half), :] for j in range(nj)], axis=1)
    mirror = jnp.dot(held, swapped, preferred_element_type=F32)
    out_ref[pl.ds(0, aux_half), :] = (early_ref[...] - mirror).astype(BF16)
    held = jnp.concatenate([other_ref[j, pl.ds(other_f, aux_half), :] for j in range(nj)], axis=1)
    straight = jnp.concatenate([t_ref[0, j] for j in range(nj)], axis=1)
    direct = lax.dot_general(
        held, straight, (((1,), (1,)), ((), ())), preferred_element_type=F32
    )
    mirror = jnp.dot(held, swapped, preferred_element_type=F32)
    out_ref[pl.ds(aux_half, aux_half), :] = (2.0 * direct - mirror).astype(BF16)


def pack_kernel(t_hbm, f_hbm, out_ref, t_ref, f_ref, sems):
    _, nj, _, block_b = t_ref.shape
    half = block_b // 2
    few = f_ref.shape[0] // 2
    load_f = pltpu.make_async_copy(f_hbm, f_ref, sems.at[0])
    load_t = pltpu.make_async_copy(t_hbm, t_ref, sems.at[1])
    load_f.start()
    load_t.start()
    load_f.wait()
    for bit in range(2):
        for side in range(2):
            piece = f_ref[pl.ds(bit * few, few), :, pl.ds(side * block_b, block_b)]
            by_j = jnp.swapaxes(piece.astype(F32), 0, 1).astype(BF16)
            for j in range(nj):
                out_ref[2 * j + bit, side, pl.ds(half, few), :] = by_j[j]
    load_t.wait()
    for bit in range(2):
        for side in range(2):
            rows = pl.ds(side * block_b + bit * half, half)
            for j in range(nj):
                out_ref[2 * j + bit, side, pl.ds(0, half), :] = t_ref[0, j, rows, :]


def project_kernel(fitted_ref, own_ref, other_ref, out_hbm, out_ref, sems):
    _, nj, _, block_b = out_ref.shape
    aux_half = fitted_ref.shape[0] // 2
    _, _, other_f = places(lax.axis_index("core"), block_b, aux_half)
    turned = fitted_ref[...].T
    stores = []
    for j in range(0, nj, 2):
        held = jnp.concatenate(
            [
                jnp.concatenate(
                    [
                        own_ref[j + i, pl.ds(block_b, aux_half), :],
                        other_ref[j + i, pl.ds(other_f, aux_half), :],
                    ],
                    axis=0,
                )
                for i in range(2)
            ],
            axis=1,
        )
        total = jnp.dot(turned, held, preferred_element_type=F32).astype(BF16)
        for i in range(2):
            out_ref[0, j + i] = total[:, i * block_b : (i + 1) * block_b]
            store = pltpu.make_async_copy(out_ref.at[0, j + i], out_hbm.at[0, j + i], sems.at[j + i])
            store.start()
            stores.append(store)
    for store in stores:
        store.wait()


def call(kernel, shapes, operands, inside=VMEM, outside=VMEM, scratch=(), dtype=BF16):
    return pl.pallas_call(
        kernel,
        out_shape=[jax.ShapeDtypeStruct(shape, dtype) for shape in shapes],
        in_specs=[inside] * len(operands),
        out_specs=[outside] * len(shapes),
        scratch_shapes=scratch,
        compiler_params=pltpu.CompilerParams(vmem_limit_bytes=32 << 20),
    )(*operands)


def body(amplitudes, factors):
    cores = lax.axis_size("core")
    chips = lax.axis_size("chip")
    cols = lax.axis_size("col")
    rows = chips * cores
    _, nj, block_a, block_b = amplitudes.shape
    block_q = factors.shape[0]
    aux = block_q * cols
    half = block_b // 2
    few = block_q // 2

    both, kept = call(
        pack_kernel,
        [(rows, 2, half + few, block_b), amplitudes.shape],
        [pltpu.with_memory_space_constraint(x, pltpu.HBM) for x in (amplitudes, factors)],
        inside=HBM,
        scratch=[pltpu.VMEM(factors.shape, BF16), pltpu.SemaphoreType.DMA((2,))],
    )
    start = ((1 - lax.axis_index("core")) * block_b).astype(jnp.uint32)
    both, start = lax.optimization_barrier((both, start))
    both = exchange(both, ROW)
    both = exchange(both.reshape(cols, half + few, block_b), "col")
    x, y = both[:, :half], both[:, half:]

    x = x.reshape(chips, 2, block_b, block_b)
    y = jnp.broadcast_to(y.reshape(1, cols * few, block_b), (chips, cols * few, block_b))
    own = exchange(jnp.concatenate([x[:, 0], y, x[:, 1]], axis=1), "chip")

    zero = jnp.uint32(0)
    other = lax.dynamic_slice(own, (zero, start, zero), (chips, block_b + aux // 2, block_b))
    other = lax.ppermute(other, "core", [(0, 1), (1, 0)])

    (early,) = call(early_kernel, [(aux // 2, block_a)], [own, kept], dtype=F32)
    (partial,) = call(fit_kernel, [(aux, block_a)], [own, other, kept, early])

    parts = exchange(partial.reshape(cols, block_q, block_a), "col")
    shard = jnp.sum(parts.astype(F32), axis=0).astype(BF16)
    copies = jnp.broadcast_to(shard[None], (cols, block_q, block_a))
    fitted = exchange(copies, "col").reshape(aux, block_a)

    (result,) = call(
        project_kernel,
        [amplitudes.shape],
        [fitted, own, other],
        outside=HBM,
        scratch=[pltpu.VMEM(amplitudes.shape, BF16), pltpu.SemaphoreType.DMA((nj,))],
    )
    return result


def solution(mesh):
    rows, cols = mesh.devices.shape
    fine = Mesh(mesh.devices.reshape(rows // 2, 2, cols), ("chip", "core", "col"))
    placed = (P(None, None, ROW, "col"), P("col", None, ROW))
    return jax.shard_map(
        body, mesh=fine, in_specs=placed, out_specs=P(None, None, ROW, "col"), check_vma=False
    )
```

```python
import jax
import jax.numpy as jnp
from jax import lax
from jax.experimental import pallas as pl
from jax.experimental.pallas import tpu as pltpu
from jax.sharding import Mesh, PartitionSpec as P

F32 = jnp.float32
BF16 = jnp.bfloat16
ROW = ("chip", "core")
VMEM = pl.BlockSpec(memory_space=pltpu.VMEM)
HBM = pl.BlockSpec(memory_space=pltpu.HBM)


def exchange(value, axes):
    return lax.all_to_all(value, axes, 0, 0, tiled=True)


def product(factors_of, own_ref, t_ref):
    _, nj, _, block_b = t_ref.shape
    half = block_b // 2
    held = jnp.concatenate([factors_of(j) for j in range(nj)], axis=1)
    straight = jnp.concatenate([t_ref[0, j] for j in range(nj)], axis=1)
    swapped = jnp.concatenate(
        [
            jnp.concatenate(
                [own_ref[i, pl.ds(side * half, half), :] for i in range(2 * nj)], axis=0
            )
            for side in range(2)
        ],
        axis=1,
    )
    direct = lax.dot_general(
        held, straight, (((1,), (1,)), ((), ())), preferred_element_type=F32
    )
    mirror = jnp.dot(held, swapped, preferred_element_type=F32)
    return (2.0 * direct - mirror).astype(BF16)


def rows_of(ref, j, start):
    size = ref.shape[1] - start
    return jnp.concatenate([ref[2 * j + i, pl.ds(start, size), :] for i in range(2)], axis=0)


def early_kernel(own_ref, t_ref, out_ref):
    start = t_ref.shape[3]
    out_ref[...] = product(lambda j: rows_of(own_ref, j, start), own_ref, t_ref)


def late_kernel(own_ref, other_ref, t_ref, early_ref, out_ref):
    count = early_ref.shape[0]
    out_ref[pl.ds(0, count), :] = early_ref[...]
    out_ref[pl.ds(count, count), :] = product(lambda j: rows_of(other_ref, j, 0), own_ref, t_ref)


def pack_kernel(t_hbm, f_hbm, out_ref, t_ref, f_ref, sems):
    _, nj, _, block_b = t_ref.shape
    half = block_b // 2
    few = f_ref.shape[0] // 2
    load_f = pltpu.make_async_copy(f_hbm, f_ref, sems.at[0])
    load_t = pltpu.make_async_copy(t_hbm, t_ref, sems.at[1])
    load_f.start()
    load_t.start()
    load_f.wait()
    for bit in range(2):
        for side in range(2):
            piece = f_ref[pl.ds(bit * few, few), :, pl.ds(side * block_b, block_b)]
            by_j = jnp.swapaxes(piece.astype(F32), 0, 1).astype(BF16)
            for j in range(nj):
                out_ref[2 * j + bit, side, pl.ds(half, few), :] = by_j[j]
    load_t.wait()
    for bit in range(2):
        for side in range(2):
            rows = pl.ds(side * block_b + bit * half, half)
            for j in range(nj):
                out_ref[2 * j + bit, side, pl.ds(0, half), :] = t_ref[0, j, rows, :]


def project_kernel(fitted_ref, own_ref, other_ref, out_hbm, out_ref, sems):
    _, nj, _, block_b = out_ref.shape
    turned = fitted_ref[...].T
    stores = []
    for j in range(0, nj, 2):
        held = jnp.concatenate(
            [
                jnp.concatenate(
                    [rows_of(own_ref, j + i, block_b), rows_of(other_ref, j + i, 0)], axis=0
                )
                for i in range(2)
            ],
            axis=1,
        )
        total = jnp.dot(turned, held, preferred_element_type=F32).astype(BF16)
        for i in range(2):
            out_ref[0, j + i] = total[:, i * block_b : (i + 1) * block_b]
            store = pltpu.make_async_copy(out_ref.at[0, j + i], out_hbm.at[0, j + i], sems.at[j + i])
            store.start()
            stores.append(store)
    for store in stores:
        store.wait()


def call(kernel, shapes, operands, inside=VMEM, outside=VMEM, scratch=()):
    return pl.pallas_call(
        kernel,
        out_shape=[jax.ShapeDtypeStruct(shape, BF16) for shape in shapes],
        in_specs=[inside] * len(operands),
        out_specs=[outside] * len(shapes),
        scratch_shapes=scratch,
        compiler_params=pltpu.CompilerParams(vmem_limit_bytes=32 << 20),
    )(*operands)


def body(amplitudes, factors):
    cores = lax.axis_size("core")
    chips = lax.axis_size("chip")
    cols = lax.axis_size("col")
    rows = chips * cores
    _, nj, block_a, block_b = amplitudes.shape
    block_q = factors.shape[0]
    aux = block_q * cols
    half = block_b // 2
    few = block_q // 2

    both, kept = call(
        pack_kernel,
        [(rows, 2, half + few, block_b), amplitudes.shape],
        [pltpu.with_memory_space_constraint(x, pltpu.HBM) for x in (amplitudes, factors)],
        inside=HBM,
        scratch=[pltpu.VMEM(factors.shape, BF16), pltpu.SemaphoreType.DMA((2,))],
    )
    both = exchange(both, ROW)
    both = exchange(both.reshape(cols, half + few, block_b), "col")
    x, y = both[:, :half], both[:, half:]

    x = x.reshape(rows, block_b, block_b)
    y = y.reshape(1, cores, aux // 4, block_b)
    y = jnp.broadcast_to(y, (chips, cores, aux // 4, block_b)).reshape(rows, aux // 4, block_b)
    own = exchange(jnp.concatenate([x, y], axis=1), ROW)

    other = lax.ppermute(own[:, block_b:], "core", [(0, 1), (1, 0)])

    (early,) = call(early_kernel, [(aux // 2, block_a)], [own, kept])
    (partial,) = call(late_kernel, [(aux, block_a)], [own, other, kept, early])

    parts = exchange(partial.reshape(cols, block_q, block_a), "col")
    shard = jnp.sum(parts.astype(F32), axis=0).astype(BF16)
    copies = jnp.broadcast_to(shard[None], (cols, block_q, block_a))
    fitted = exchange(copies, "col").reshape(aux, block_a)

    (result,) = call(
        project_kernel,
        [amplitudes.shape],
        [fitted, own, other],
        outside=HBM,
        scratch=[pltpu.VMEM(amplitudes.shape, BF16), pltpu.SemaphoreType.DMA((nj,))],
    )
    return result


def solution(mesh):
    rows, cols = mesh.devices.shape
    fine = Mesh(mesh.devices.reshape(rows // 2, 2, cols), ("chip", "core", "col"))
    placed = (P(None, None, ROW, "col"), P("col", None, ROW))
    return jax.shard_map(
        body, mesh=fine, in_specs=placed, out_specs=P(None, None, ROW, "col"), check_vma=False
    )
```

```python
import jax
import jax.numpy as jnp
from jax import lax
from jax.experimental import pallas as pl
from jax.experimental.pallas import tpu as pltpu
from jax.sharding import Mesh, PartitionSpec as P

F32 = jnp.float32
BF16 = jnp.bfloat16
ROW = ("chip", "core")
VMEM = pl.BlockSpec(memory_space=pltpu.VMEM)
HBM = pl.BlockSpec(memory_space=pltpu.HBM)


def exchange(value, axes):
    return lax.all_to_all(value, axes, 0, 0, tiled=True)


def places(core, block_b, aux_half):
    own_t = pl.multiple_of(core * (block_b + aux_half), block_b)
    other_t = pl.multiple_of(core * aux_half, block_b)
    other_f = pl.multiple_of((1 - core) * block_b, block_b)
    return own_t, other_t, other_f


def early_kernel(own_ref, t_ref, out_ref):
    _, nj, _, block_b = t_ref.shape
    aux_half = out_ref.shape[0]
    held = jnp.concatenate([own_ref[j, pl.ds(block_b, aux_half), :] for j in range(nj)], axis=1)
    straight = jnp.concatenate([t_ref[0, j] for j in range(nj)], axis=1)
    out_ref[...] = 2.0 * lax.dot_general(
        held, straight, (((1,), (1,)), ((), ())), preferred_element_type=F32
    )


def fit_kernel(own_ref, other_ref, t_ref, early_ref, out_ref):
    _, nj, block_a, block_b = t_ref.shape
    half = block_b // 2
    aux_half = out_ref.shape[0] // 2
    core = lax.axis_index("core")
    own_t, other_t, other_f = places(core, block_b, aux_half)
    columns = []
    for side in range(2):
        blocks = []
        for j in range(nj):
            mine = own_ref[j, pl.ds(own_t + side * half, half), :]
            theirs = other_ref[j, pl.ds(other_t + side * half, half), :]
            blocks.append(jnp.where(core == 0, mine, theirs))
            blocks.append(jnp.where(core == 0, theirs, mine))
        columns.append(jnp.concatenate(blocks, axis=0))
    swapped = jnp.concatenate(columns, axis=1)
    held = jnp.concatenate([own_ref[j, pl.ds(block_b, aux_half), :] for j in range(nj)], axis=1)
    mirror = jnp.dot(held, swapped, preferred_element_type=F32)
    out_ref[pl.ds(0, aux_half), :] = (early_ref[...] - mirror).astype(BF16)
    held = jnp.concatenate([other_ref[j, pl.ds(other_f, aux_half), :] for j in range(nj)], axis=1)
    straight = jnp.concatenate([t_ref[0, j] for j in range(nj)], axis=1)
    direct = lax.dot_general(
        held, straight, (((1,), (1,)), ((), ())), preferred_element_type=F32
    )
    mirror = jnp.dot(held, swapped, preferred_element_type=F32)
    out_ref[pl.ds(aux_half, aux_half), :] = (2.0 * direct - mirror).astype(BF16)


def pack_kernel(t_hbm, f_hbm, out_ref, t_ref, f_ref, sems):
    _, nj, _, block_b = t_ref.shape
    half = block_b // 2
    few = f_ref.shape[0] // 2
    load_f = pltpu.make_async_copy(f_hbm, f_ref, sems.at[0])
    load_t = pltpu.make_async_copy(t_hbm, t_ref, sems.at[1])
    load_f.start()
    load_t.start()
    load_f.wait()
    for bit in range(2):
        for side in range(2):
            piece = f_ref[pl.ds(bit * few, few), :, pl.ds(side * block_b, block_b)]
            by_j = jnp.swapaxes(piece.astype(F32), 0, 1).astype(BF16)
            for j in range(nj):
                out_ref[2 * j + bit, side, pl.ds(half, few), :] = by_j[j]
    load_t.wait()
    for bit in range(2):
        for side in range(2):
            rows = pl.ds(side * block_b + bit * half, half)
            for j in range(nj):
                out_ref[2 * j + bit, side, pl.ds(0, half), :] = t_ref[0, j, rows, :]


def spread_kernel(both_ref, out_ref):
    chips, _, block_b = out_ref.shape
    half = block_b // 2
    count = both_ref.shape[0]
    per_chip = count // chips
    few = both_ref.shape[1] - half
    factors = both_ref[:, pl.ds(half, few), :].reshape(count * few, block_b)
    for chip in range(chips):
        out_ref[chip, pl.ds(block_b, count * few), :] = factors
        for i in range(per_chip):
            place = i * half + (i // 2) * count * few
            out_ref[chip, pl.ds(place, half), :] = both_ref[chip * per_chip + i, pl.ds(0, half), :]


def sum_kernel(parts_ref, out_ref):
    total = jnp.sum(parts_ref[...].astype(F32), axis=0).astype(BF16)
    out_ref[...] = jnp.broadcast_to(total[None], out_ref.shape)


def project_kernel(fitted_ref, own_ref, other_ref, out_hbm, out_ref, sems):
    _, nj, _, block_b = out_ref.shape
    aux_half = fitted_ref.shape[0] // 2
    _, _, other_f = places(lax.axis_index("core"), block_b, aux_half)
    turned = fitted_ref[...].T
    stores = []
    for j in range(0, nj, 2):
        held = jnp.concatenate(
            [
                jnp.concatenate(
                    [
                        own_ref[j + i, pl.ds(block_b, aux_half), :],
                        other_ref[j + i, pl.ds(other_f, aux_half), :],
                    ],
                    axis=0,
                )
                for i in range(2)
            ],
            axis=1,
        )
        total = jnp.dot(turned, held, preferred_element_type=F32).astype(BF16)
        for i in range(2):
            out_ref[0, j + i] = total[:, i * block_b : (i + 1) * block_b]
            store = pltpu.make_async_copy(out_ref.at[0, j + i], out_hbm.at[0, j + i], sems.at[j + i])
            store.start()
            stores.append(store)
    for store in stores:
        store.wait()


def call(kernel, shapes, operands, inside=VMEM, outside=VMEM, scratch=(), dtype=BF16):
    return pl.pallas_call(
        kernel,
        out_shape=[jax.ShapeDtypeStruct(shape, dtype) for shape in shapes],
        in_specs=[inside] * len(operands),
        out_specs=[outside] * len(shapes),
        scratch_shapes=scratch,
        compiler_params=pltpu.CompilerParams(vmem_limit_bytes=32 << 20),
    )(*operands)


def body(amplitudes, factors):
    cores = lax.axis_size("core")
    chips = lax.axis_size("chip")
    cols = lax.axis_size("col")
    rows = chips * cores
    _, nj, block_a, block_b = amplitudes.shape
    block_q = factors.shape[0]
    aux = block_q * cols
    half = block_b // 2
    few = block_q // 2

    both, kept = call(
        pack_kernel,
        [(rows, 2, half + few, block_b), amplitudes.shape],
        [pltpu.with_memory_space_constraint(x, pltpu.HBM) for x in (amplitudes, factors)],
        inside=HBM,
        scratch=[pltpu.VMEM(factors.shape, BF16), pltpu.SemaphoreType.DMA((2,))],
    )
    start = ((1 - lax.axis_index("core")) * block_b).astype(jnp.uint32)
    both, start = lax.optimization_barrier((both, start))
    both = exchange(both, ROW)
    both = exchange(both.reshape(cols, half + few, block_b), "col")

    (both,) = call(spread_kernel, [(chips, 2 * block_b + aux // 2, block_b)], [both])
    own = exchange(both, "chip")

    zero = jnp.uint32(0)
    other = lax.dynamic_slice(own, (zero, start, zero), (chips, block_b + aux // 2, block_b))
    other = lax.ppermute(other, "core", [(0, 1), (1, 0)])

    (early,) = call(early_kernel, [(aux // 2, block_a)], [own, kept], dtype=F32)
    (partial,) = call(fit_kernel, [(aux, block_a)], [own, other, kept, early])

    parts = exchange(partial.reshape(cols, block_q, block_a), "col")
    (copies,) = call(sum_kernel, [parts.shape], [parts])
    fitted = exchange(copies, "col").reshape(aux, block_a)

    (result,) = call(
        project_kernel,
        [amplitudes.shape],
        [fitted, own, other],
        outside=HBM,
        scratch=[pltpu.VMEM(amplitudes.shape, BF16), pltpu.SemaphoreType.DMA((nj,))],
    )
    return result


def solution(mesh):
    rows, cols = mesh.devices.shape
    fine = Mesh(mesh.devices.reshape(rows // 2, 2, cols), ("chip", "core", "col"))
    placed = (P(None, None, ROW, "col"), P("col", None, ROW))
    return jax.shard_map(
        body, mesh=fine, in_specs=placed, out_specs=P(None, None, ROW, "col"), check_vma=False
    )
```

```python
import jax
import jax.numpy as jnp
from jax import lax
from jax.experimental import pallas as pl
from jax.experimental.pallas import tpu as pltpu
from jax.sharding import Mesh, PartitionSpec as P

F32 = jnp.float32
BF16 = jnp.bfloat16
ROW = ("chip", "core")
COL = ("y", "z")
VMEM = pl.BlockSpec(memory_space=pltpu.VMEM)
HBM = pl.BlockSpec(memory_space=pltpu.HBM)


def exchange(value, axes):
    return lax.all_to_all(value, axes, 0, 0, tiled=True)


def places(core, block_b, aux_half):
    own_t = pl.multiple_of(core * (block_b + aux_half), block_b)
    other_t = pl.multiple_of(core * aux_half, block_b)
    other_f = pl.multiple_of((1 - core) * block_b, block_b)
    return own_t, other_t, other_f


def early_kernel(own_ref, t_ref, out_ref):
    _, nj, _, block_b = t_ref.shape
    aux_half = out_ref.shape[0]
    held = jnp.concatenate([own_ref[j, pl.ds(block_b, aux_half), :] for j in range(nj)], axis=1)
    straight = jnp.concatenate([t_ref[0, j] for j in range(nj)], axis=1)
    out_ref[...] = 2.0 * lax.dot_general(
        held, straight, (((1,), (1,)), ((), ())), preferred_element_type=F32
    )


def fit_kernel(own_ref, other_ref, t_ref, early_ref, out_ref):
    _, nj, block_a, block_b = t_ref.shape
    half = block_b // 2
    aux_half = out_ref.shape[0] // 2
    core = lax.axis_index("core")
    own_t, other_t, other_f = places(core, block_b, aux_half)
    columns = []
    for side in range(2):
        blocks = []
        for j in range(nj):
            mine = own_ref[j, pl.ds(own_t + side * half, half), :]
            theirs = other_ref[j, pl.ds(other_t + side * half, half), :]
            blocks.append(jnp.where(core == 0, mine, theirs))
            blocks.append(jnp.where(core == 0, theirs, mine))
        columns.append(jnp.concatenate(blocks, axis=0))
    swapped = jnp.concatenate(columns, axis=1)
    held = jnp.concatenate([own_ref[j, pl.ds(block_b, aux_half), :] for j in range(nj)], axis=1)
    mirror = jnp.dot(held, swapped, preferred_element_type=F32)
    out_ref[pl.ds(0, aux_half), :] = (early_ref[...] - mirror).astype(BF16)
    held = jnp.concatenate([other_ref[j, pl.ds(other_f, aux_half), :] for j in range(nj)], axis=1)
    straight = jnp.concatenate([t_ref[0, j] for j in range(nj)], axis=1)
    direct = lax.dot_general(
        held, straight, (((1,), (1,)), ((), ())), preferred_element_type=F32
    )
    mirror = jnp.dot(held, swapped, preferred_element_type=F32)
    out_ref[pl.ds(aux_half, aux_half), :] = (2.0 * direct - mirror).astype(BF16)


def pack_kernel(t_hbm, f_hbm, out_ref, t_ref, f_ref, sems):
    _, nj, _, block_b = t_ref.shape
    half = block_b // 2
    few = f_ref.shape[0] // 2
    load_f = pltpu.make_async_copy(f_hbm, f_ref, sems.at[0])
    load_t = pltpu.make_async_copy(t_hbm, t_ref, sems.at[1])
    load_f.start()
    load_t.start()
    load_f.wait()
    for bit in range(2):
        for side in range(2):
            piece = f_ref[pl.ds(bit * few, few), :, pl.ds(side * block_b, block_b)]
            by_j = jnp.swapaxes(piece.astype(F32), 0, 1).astype(BF16)
            for j in range(nj):
                out_ref[2 * j + bit, side, pl.ds(half, few), :] = by_j[j]
    load_t.wait()
    for bit in range(2):
        for side in range(2):
            rows = pl.ds(side * block_b + bit * half, half)
            for j in range(nj):
                out_ref[2 * j + bit, side, pl.ds(0, half), :] = t_ref[0, j, rows, :]


def project_kernel(fitted_ref, own_ref, other_ref, out_hbm, out_ref, sems):
    _, nj, _, block_b = out_ref.shape
    aux_half = fitted_ref.shape[0] // 2
    _, _, other_f = places(lax.axis_index("core"), block_b, aux_half)
    turned = fitted_ref[...].T
    stores = []
    for j in range(0, nj, 2):
        held = jnp.concatenate(
            [
                jnp.concatenate(
                    [
                        own_ref[j + i, pl.ds(block_b, aux_half), :],
                        other_ref[j + i, pl.ds(other_f, aux_half), :],
                    ],
                    axis=0,
                )
                for i in range(2)
            ],
            axis=1,
        )
        total = jnp.dot(turned, held, preferred_element_type=F32).astype(BF16)
        for i in range(2):
            out_ref[0, j + i] = total[:, i * block_b : (i + 1) * block_b]
            store = pltpu.make_async_copy(out_ref.at[0, j + i], out_hbm.at[0, j + i], sems.at[j + i])
            store.start()
            stores.append(store)
    for store in stores:
        store.wait()


def call(kernel, shapes, operands, inside=VMEM, outside=VMEM, scratch=(), dtype=BF16):
    return pl.pallas_call(
        kernel,
        out_shape=[jax.ShapeDtypeStruct(shape, dtype) for shape in shapes],
        in_specs=[inside] * len(operands),
        out_specs=[outside] * len(shapes),
        scratch_shapes=scratch,
        compiler_params=pltpu.CompilerParams(vmem_limit_bytes=32 << 20),
    )(*operands)


def body(amplitudes, factors):
    cores = lax.axis_size("core")
    chips = lax.axis_size("chip")
    along_y, along_z = lax.axis_size("y"), lax.axis_size("z")
    cols = along_y * along_z
    rows = chips * cores
    _, nj, block_a, block_b = amplitudes.shape
    block_q = factors.shape[0]
    aux = block_q * cols
    half = block_b // 2
    few = block_q // 2

    both, kept = call(
        pack_kernel,
        [(rows, 2, half + few, block_b), amplitudes.shape],
        [pltpu.with_memory_space_constraint(x, pltpu.HBM) for x in (amplitudes, factors)],
        inside=HBM,
        scratch=[pltpu.VMEM(factors.shape, BF16), pltpu.SemaphoreType.DMA((2,))],
    )
    start = ((1 - lax.axis_index("core")) * block_b).astype(jnp.uint32)
    both, start = lax.optimization_barrier((both, start))
    both = exchange(both, ROW)
    both = exchange(both.reshape(cols, half + few, block_b), COL)
    x, y = both[:, :half], both[:, half:]

    x = x.reshape(chips, 2, block_b, block_b)
    y = jnp.broadcast_to(y.reshape(1, cols * few, block_b), (chips, cols * few, block_b))
    own = exchange(jnp.concatenate([x[:, 0], y, x[:, 1]], axis=1), "chip")

    zero = jnp.uint32(0)
    other = lax.dynamic_slice(own, (zero, start, zero), (chips, block_b + aux // 2, block_b))
    other = lax.ppermute(other, "core", [(0, 1), (1, 0)])

    (early,) = call(early_kernel, [(aux // 2, block_a)], [own, kept], dtype=F32)
    (partial,) = call(fit_kernel, [(aux, block_a)], [own, other, kept, early])

    parts = exchange(partial.reshape(cols, block_q, block_a), ("z", "y"))
    shard = jnp.sum(parts.astype(F32), axis=0).astype(BF16)
    copies = jnp.broadcast_to(shard[None], (along_y, block_q, block_a))
    some = exchange(copies, "y").reshape(1, along_y * block_q, block_a)
    copies = jnp.broadcast_to(some, (along_z, along_y * block_q, block_a))
    fitted = exchange(copies, "z").reshape(aux, block_a)

    (result,) = call(
        project_kernel,
        [amplitudes.shape],
        [fitted, own, other],
        outside=HBM,
        scratch=[pltpu.VMEM(amplitudes.shape, BF16), pltpu.SemaphoreType.DMA((nj,))],
    )
    return result


def solution(mesh):
    rows, cols = mesh.devices.shape
    fine = Mesh(mesh.devices.reshape(rows // 2, 2, cols // 4, 4), ROW + COL)
    placed = (P(None, None, ROW, COL), P(COL, None, ROW))
    return jax.shard_map(
        body, mesh=fine, in_specs=placed, out_specs=P(None, None, ROW, COL), check_vma=False
    )
```

```python
import jax
import jax.numpy as jnp
from jax import lax
from jax.experimental import pallas as pl
from jax.experimental.pallas import tpu as pltpu
from jax.sharding import Mesh, PartitionSpec as P

F32 = jnp.float32
BF16 = jnp.bfloat16
ROW = ("chip", "core")
VMEM = pl.BlockSpec(memory_space=pltpu.VMEM)
HBM = pl.BlockSpec(memory_space=pltpu.HBM)


def exchange(value, axes):
    return lax.all_to_all(value, axes, 0, 0, tiled=True)


def places(core, block_b, aux_half):
    own_t = pl.multiple_of(core * (block_b + aux_half), block_b)
    other_t = pl.multiple_of(core * aux_half, block_b)
    other_f = pl.multiple_of((1 - core) * block_b, block_b)
    return own_t, other_t, other_f


def early_kernel(own_ref, t_ref, out_ref):
    _, nj, _, block_b = t_ref.shape
    aux_half = out_ref.shape[0]
    held = jnp.concatenate([own_ref[j, pl.ds(block_b, aux_half), :] for j in range(nj)], axis=1)
    straight = jnp.concatenate([t_ref[0, j] for j in range(nj)], axis=1)
    out_ref[...] = 2.0 * lax.dot_general(
        held, straight, (((1,), (1,)), ((), ())), preferred_element_type=F32
    )


def fit_kernel(own_ref, other_ref, t_ref, early_ref, out_ref):
    _, nj, block_a, block_b = t_ref.shape
    half = block_b // 2
    aux_half = out_ref.shape[0] // 2
    core = lax.axis_index("core")
    own_t, other_t, other_f = places(core, block_b, aux_half)
    columns = []
    for side in range(2):
        blocks = []
        for j in range(nj):
            mine = own_ref[j, pl.ds(own_t + side * half, half), :]
            theirs = other_ref[j, pl.ds(other_t + side * half, half), :]
            blocks.append(jnp.where(core == 0, mine, theirs))
            blocks.append(jnp.where(core == 0, theirs, mine))
        columns.append(jnp.concatenate(blocks, axis=0))
    swapped = jnp.concatenate(columns, axis=1)
    held = jnp.concatenate([own_ref[j, pl.ds(block_b, aux_half), :] for j in range(nj)], axis=1)
    mirror = jnp.dot(held, swapped, preferred_element_type=F32)
    out_ref[pl.ds(0, aux_half), :] = (early_ref[...] - mirror).astype(BF16)
    held = jnp.concatenate([other_ref[j, pl.ds(other_f, aux_half), :] for j in range(nj)], axis=1)
    straight = jnp.concatenate([t_ref[0, j] for j in range(nj)], axis=1)
    direct = lax.dot_general(
        held, straight, (((1,), (1,)), ((), ())), preferred_element_type=F32
    )
    mirror = jnp.dot(held, swapped, preferred_element_type=F32)
    out_ref[pl.ds(aux_half, aux_half), :] = (2.0 * direct - mirror).astype(BF16)


def pack_kernel(t_hbm, f_hbm, out_ref, t_ref, f_ref, sems):
    _, nj, _, block_b = t_ref.shape
    half = block_b // 2
    few = f_ref.shape[0] // 2
    load_f = pltpu.make_async_copy(f_hbm, f_ref, sems.at[0])
    load_t = pltpu.make_async_copy(t_hbm, t_ref, sems.at[1])
    load_f.start()
    load_t.start()
    load_f.wait()
    for bit in range(2):
        for side in range(2):
            piece = f_ref[pl.ds(bit * few, few), :, pl.ds(side * block_b, block_b)]
            by_j = jnp.swapaxes(piece.astype(F32), 0, 1).astype(BF16)
            for j in range(nj):
                out_ref[2 * j + bit, side, pl.ds(half, few), :] = by_j[j]
    load_t.wait()
    for bit in range(2):
        for side in range(2):
            rows = pl.ds(side * block_b + bit * half, half)
            for j in range(nj):
                out_ref[2 * j + bit, side, pl.ds(0, half), :] = t_ref[0, j, rows, :]


def project_kernel(fitted_ref, own_ref, other_ref, out_hbm, out_ref, sems):
    _, nj, _, block_b = out_ref.shape
    aux_half = fitted_ref.shape[0] // 2
    _, _, other_f = places(lax.axis_index("core"), block_b, aux_half)
    turned = fitted_ref[...].T
    stores = []
    for j in range(0, nj, 2):
        held = jnp.concatenate(
            [
                jnp.concatenate(
                    [
                        own_ref[j + i, pl.ds(block_b, aux_half), :],
                        other_ref[j + i, pl.ds(other_f, aux_half), :],
                    ],
                    axis=0,
                )
                for i in range(2)
            ],
            axis=1,
        )
        total = jnp.dot(turned, held, preferred_element_type=F32).astype(BF16)
        for i in range(2):
            out_ref[0, j + i] = total[:, i * block_b : (i + 1) * block_b]
            store = pltpu.make_async_copy(out_ref.at[0, j + i], out_hbm.at[0, j + i], sems.at[j + i])
            store.start()
            stores.append(store)
    for store in stores:
        store.wait()


def call(kernel, shapes, operands, inside=VMEM, outside=VMEM, scratch=(), dtype=BF16):
    return pl.pallas_call(
        kernel,
        out_shape=[jax.ShapeDtypeStruct(shape, dtype) for shape in shapes],
        in_specs=[inside] * len(operands),
        out_specs=[outside] * len(shapes),
        scratch_shapes=scratch,
        compiler_params=pltpu.CompilerParams(vmem_limit_bytes=32 << 20),
    )(*operands)


def body(amplitudes, factors):
    cores = lax.axis_size("core")
    chips = lax.axis_size("chip")
    cols = lax.axis_size("col")
    rows = chips * cores
    _, nj, block_a, block_b = amplitudes.shape
    block_q = factors.shape[0]
    aux = block_q * cols
    half = block_b // 2
    few = block_q // 2

    both, kept = call(
        pack_kernel,
        [(rows, 2, half + few, block_b), amplitudes.shape],
        [pltpu.with_memory_space_constraint(x, pltpu.HBM) for x in (amplitudes, factors)],
        inside=HBM,
        scratch=[pltpu.VMEM(factors.shape, BF16), pltpu.SemaphoreType.DMA((2,))],
    )
    start = ((1 - lax.axis_index("core")) * block_b).astype(jnp.uint32)
    both, start = lax.optimization_barrier((both, start))
    both = exchange(both, ROW)
    both = exchange(both.reshape(cols, half + few, block_b), "col")
    x, y = both[:, :half], both[:, half:]

    x = x.reshape(chips, 2, block_b, block_b)
    y = jnp.broadcast_to(y.reshape(1, cols * few, block_b), (chips, cols * few, block_b))
    own = exchange(jnp.concatenate([x[:, 0], y, x[:, 1]], axis=1), "chip")

    zero = jnp.uint32(0)
    other = lax.dynamic_slice(own, (zero, start, zero), (chips, block_b + aux // 2, block_b))
    other = lax.ppermute(other, "core", [(0, 1), (1, 0)])

    (early,) = call(early_kernel, [(aux // 2, block_a)], [own, kept], dtype=F32)
    (partial,) = call(fit_kernel, [(aux, block_a)], [own, other, kept, early])

    group = ("core", "col")
    block = (block_q // cores, block_a)
    parts = exchange(partial.reshape((cores * cols,) + block), group)
    shards = jnp.sum(parts.reshape((cores, cols) + block).astype(F32), axis=1).astype(BF16)
    copies = jnp.broadcast_to(shards[:, None], (cores, cols) + block)
    fitted = exchange(copies.reshape((cores * cols,) + block), group).reshape(aux, block_a)

    (result,) = call(
        project_kernel,
        [amplitudes.shape],
        [fitted, own, other],
        outside=HBM,
        scratch=[pltpu.VMEM(amplitudes.shape, BF16), pltpu.SemaphoreType.DMA((nj,))],
    )
    return result


def solution(mesh):
    rows, cols = mesh.devices.shape
    fine = Mesh(mesh.devices.reshape(rows // 2, 2, cols), ("chip", "core", "col"))
    placed = (P(None, None, ROW, "col"), P("col", None, ROW))
    return jax.shard_map(
        body, mesh=fine, in_specs=placed, out_specs=P(None, None, ROW, "col"), check_vma=False
    )
```

```python
import jax
import jax.numpy as jnp
from jax import lax
from jax.experimental import pallas as pl
from jax.experimental.pallas import tpu as pltpu
from jax.sharding import Mesh, PartitionSpec as P

F32 = jnp.float32
BF16 = jnp.bfloat16
ROW = ("chip", "core")
VMEM = pl.BlockSpec(memory_space=pltpu.VMEM)
HBM = pl.BlockSpec(memory_space=pltpu.HBM)


def exchange(value, axes):
    return lax.all_to_all(value, axes, 0, 0, tiled=True)


def product(held_ref, first, count, own_ref, other_ref, t_ref):
    _, nj, _, block_b = t_ref.shape
    half = block_b // 2
    core = lax.axis_index("core")
    own_t = pl.multiple_of(core * (own_ref.shape[1] - block_b), block_b)
    columns = []
    for side in range(2):
        blocks = []
        for j in range(nj):
            mine = own_ref[j, pl.ds(own_t + side * half, half), :]
            theirs = other_ref[j, pl.ds(side * half, half), :]
            blocks.append(jnp.where(core == 0, mine, theirs))
            blocks.append(jnp.where(core == 0, theirs, mine))
        columns.append(jnp.concatenate(blocks, axis=0))
    swapped = jnp.concatenate(columns, axis=1)
    straight = jnp.concatenate([t_ref[0, j] for j in range(nj)], axis=1)
    held = jnp.concatenate([held_ref[j, pl.ds(first, count), :] for j in range(nj)], axis=1)
    direct = lax.dot_general(
        held, straight, (((1,), (1,)), ((), ())), preferred_element_type=F32
    )
    mirror = jnp.dot(held, swapped, preferred_element_type=F32)
    return (2.0 * direct - mirror).astype(BF16)


def early_kernel(own_ref, other_ref, t_ref, out_ref):
    out_ref[...] = product(own_ref, t_ref.shape[3], out_ref.shape[0], own_ref, other_ref, t_ref)


def late_kernel(own_ref, other_ref, factors_ref, t_ref, early_ref, out_ref):
    count = early_ref.shape[0]
    out_ref[pl.ds(0, count), :] = early_ref[...]
    out_ref[pl.ds(count, count), :] = product(factors_ref, 0, count, own_ref, other_ref, t_ref)


def pack_kernel(t_hbm, f_hbm, out_ref, t_ref, f_ref, sems):
    _, nj, _, block_b = t_ref.shape
    half = block_b // 2
    few = f_ref.shape[0] // 2
    load_f = pltpu.make_async_copy(f_hbm, f_ref, sems.at[0])
    load_t = pltpu.make_async_copy(t_hbm, t_ref, sems.at[1])
    load_f.start()
    load_t.start()
    load_f.wait()
    for bit in range(2):
        for side in range(2):
            piece = f_ref[pl.ds(bit * few, few), :, pl.ds(side * block_b, block_b)]
            by_j = jnp.swapaxes(piece.astype(F32), 0, 1).astype(BF16)
            for j in range(nj):
                out_ref[2 * j + bit, side, pl.ds(half, few), :] = by_j[j]
    load_t.wait()
    for bit in range(2):
        for side in range(2):
            rows = pl.ds(side * block_b + bit * half, half)
            for j in range(nj):
                out_ref[2 * j + bit, side, pl.ds(0, half), :] = t_ref[0, j, rows, :]


def project_kernel(fitted_ref, own_ref, other_ref, out_hbm, out_ref, sems):
    _, nj, _, block_b = out_ref.shape
    aux_half = fitted_ref.shape[0] // 2
    turned = fitted_ref[...].T
    stores = []
    for j in range(0, nj, 2):
        held = jnp.concatenate(
            [
                jnp.concatenate(
                    [
                        own_ref[j + i, pl.ds(block_b, aux_half), :],
                        other_ref[j + i],
                    ],
                    axis=0,
                )
                for i in range(2)
            ],
            axis=1,
        )
        total = jnp.dot(turned, held, preferred_element_type=F32).astype(BF16)
        for i in range(2):
            out_ref[0, j + i] = total[:, i * block_b : (i + 1) * block_b]
            store = pltpu.make_async_copy(out_ref.at[0, j + i], out_hbm.at[0, j + i], sems.at[j + i])
            store.start()
            stores.append(store)
    for store in stores:
        store.wait()


def call(kernel, shapes, operands, inside=VMEM, outside=VMEM, scratch=()):
    return pl.pallas_call(
        kernel,
        out_shape=[jax.ShapeDtypeStruct(shape, BF16) for shape in shapes],
        in_specs=[inside] * len(operands),
        out_specs=[outside] * len(shapes),
        scratch_shapes=scratch,
        compiler_params=pltpu.CompilerParams(vmem_limit_bytes=32 << 20),
    )(*operands)


def body(amplitudes, factors):
    cores = lax.axis_size("core")
    chips = lax.axis_size("chip")
    cols = lax.axis_size("col")
    rows = chips * cores
    _, nj, block_a, block_b = amplitudes.shape
    block_q = factors.shape[0]
    aux = block_q * cols
    half = block_b // 2
    few = block_q // 2

    both, kept = call(
        pack_kernel,
        [(rows, 2, half + few, block_b), amplitudes.shape],
        [pltpu.with_memory_space_constraint(x, pltpu.HBM) for x in (amplitudes, factors)],
        inside=HBM,
        scratch=[pltpu.VMEM(factors.shape, BF16), pltpu.SemaphoreType.DMA((2,))],
    )
    start = ((1 - lax.axis_index("core")) * (block_b + aux // 2)).astype(jnp.uint32)
    both, start = lax.optimization_barrier((both, start))
    both = exchange(both, ROW)
    both = exchange(both.reshape(cols, half + few, block_b), "col")
    x, y = both[:, :half], both[:, half:]

    x = x.reshape(chips, 2, block_b, block_b)
    y = jnp.broadcast_to(y.reshape(1, cols * few, block_b), (chips, cols * few, block_b))
    own = exchange(jnp.concatenate([x[:, 0], y, x[:, 1]], axis=1), "chip")

    zero = jnp.uint32(0)
    swap = [(0, 1), (1, 0)]
    sent = lax.dynamic_slice(own, (zero, start, zero), (chips, block_b, block_b))
    turned = lax.ppermute(sent, "core", swap)
    other = lax.ppermute(own[:, block_b : block_b + aux // 2], "core", swap)

    (early,) = call(early_kernel, [(aux // 2, block_a)], [own, turned, kept])
    (partial,) = call(late_kernel, [(aux, block_a)], [own, turned, other, kept, early])

    parts = exchange(partial.reshape(cols, block_q, block_a), "col")
    shard = jnp.sum(parts.astype(F32), axis=0).astype(BF16)
    copies = jnp.broadcast_to(shard[None], (cols, block_q, block_a))
    fitted = exchange(copies, "col").reshape(aux, block_a)

    (result,) = call(
        project_kernel,
        [amplitudes.shape],
        [fitted, own, other],
        outside=HBM,
        scratch=[pltpu.VMEM(amplitudes.shape, BF16), pltpu.SemaphoreType.DMA((nj,))],
    )
    return result


def solution(mesh):
    rows, cols = mesh.devices.shape
    fine = Mesh(mesh.devices.reshape(rows // 2, 2, cols), ("chip", "core", "col"))
    placed = (P(None, None, ROW, "col"), P("col", None, ROW))
    return jax.shard_map(
        body, mesh=fine, in_specs=placed, out_specs=P(None, None, ROW, "col"), check_vma=False
    )
```

```python
import jax
import jax.numpy as jnp
from jax import lax
from jax.experimental import pallas as pl
from jax.experimental.pallas import tpu as pltpu
from jax.sharding import Mesh, PartitionSpec as P

F32 = jnp.float32
BF16 = jnp.bfloat16
ROW = ("chip", "core")
VMEM = pl.BlockSpec(memory_space=pltpu.VMEM)
HBM = pl.BlockSpec(memory_space=pltpu.HBM)


def exchange(value, axes):
    return lax.all_to_all(value, axes, 0, 0, tiled=True)


def places(core, block_b, aux_half):
    own_t = pl.multiple_of(core * (block_b + aux_half), block_b)
    other_t = pl.multiple_of(core * aux_half, block_b)
    other_f = pl.multiple_of((1 - core) * block_b, block_b)
    return own_t, other_t, other_f


def early_kernel(own_ref, t_ref, out_ref):
    _, nj, _, block_b = t_ref.shape
    aux_half = out_ref.shape[0]
    held = jnp.concatenate([own_ref[j, pl.ds(block_b, aux_half), :] for j in range(nj)], axis=1)
    straight = jnp.concatenate([t_ref[0, j] for j in range(nj)], axis=1)
    out_ref[...] = 2.0 * lax.dot_general(
        held, straight, (((1,), (1,)), ((), ())), preferred_element_type=F32
    )


def fit_kernel(own_ref, other_ref, t_ref, early_ref, out_ref):
    _, nj, block_a, block_b = t_ref.shape
    half = block_b // 2
    aux_half = out_ref.shape[0] // 2
    core = lax.axis_index("core")
    own_t, other_t, other_f = places(core, block_b, aux_half)
    columns = []
    for side in range(2):
        blocks = []
        for j in range(nj):
            mine = own_ref[j, pl.ds(own_t + side * half, half), :]
            theirs = other_ref[j, pl.ds(other_t + side * half, half), :]
            blocks.append(jnp.where(core == 0, mine, theirs))
            blocks.append(jnp.where(core == 0, theirs, mine))
        columns.append(jnp.concatenate(blocks, axis=0))
    swapped = jnp.concatenate(columns, axis=1)
    held = jnp.concatenate([own_ref[j, pl.ds(block_b, aux_half), :] for j in range(nj)], axis=1)
    mirror = jnp.dot(held, swapped, preferred_element_type=F32)
    out_ref[pl.ds(0, aux_half), :] = (early_ref[...] - mirror).astype(BF16)
    held = jnp.concatenate([other_ref[j, pl.ds(other_f, aux_half), :] for j in range(nj)], axis=1)
    straight = jnp.concatenate([t_ref[0, j] for j in range(nj)], axis=1)
    direct = lax.dot_general(
        held, straight, (((1,), (1,)), ((), ())), preferred_element_type=F32
    )
    mirror = jnp.dot(held, swapped, preferred_element_type=F32)
    out_ref[pl.ds(aux_half, aux_half), :] = (2.0 * direct - mirror).astype(BF16)


def pack_kernel(t_hbm, f_hbm, out_ref, t_ref, f_ref, sems):
    _, nj, _, block_b = t_ref.shape
    half = block_b // 2
    few = f_ref.shape[0] // 2
    load_f = pltpu.make_async_copy(f_hbm, f_ref, sems.at[0])
    load_t = pltpu.make_async_copy(t_hbm, t_ref, sems.at[1])
    load_f.start()
    load_t.start()
    load_f.wait()
    for bit in range(2):
        for side in range(2):
            piece = f_ref[pl.ds(bit * few, few), :, pl.ds(side * block_b, block_b)]
            by_j = jnp.swapaxes(piece.astype(F32), 0, 1).astype(BF16)
            for j in range(nj):
                out_ref[2 * j + bit, side, pl.ds(half, few), :] = by_j[j]
    load_t.wait()
    for bit in range(2):
        for side in range(2):
            rows = pl.ds(side * block_b + bit * half, half)
            for j in range(nj):
                out_ref[2 * j + bit, side, pl.ds(0, half), :] = t_ref[0, j, rows, :]


def sum_kernel(parts_ref, out_ref):
    total = jnp.sum(parts_ref[...].astype(F32), axis=0).astype(BF16)
    out_ref[...] = jnp.broadcast_to(total[None], out_ref.shape)


def project_kernel(fitted_ref, own_ref, other_ref, out_hbm, out_ref, sems):
    _, nj, _, block_b = out_ref.shape
    aux_half = fitted_ref.shape[0] // 2
    _, _, other_f = places(lax.axis_index("core"), block_b, aux_half)
    turned = fitted_ref[...].T
    stores = []
    for j in range(0, nj, 2):
        held = jnp.concatenate(
            [
                jnp.concatenate(
                    [
                        own_ref[j + i, pl.ds(block_b, aux_half), :],
                        other_ref[j + i, pl.ds(other_f, aux_half), :],
                    ],
                    axis=0,
                )
                for i in range(2)
            ],
            axis=1,
        )
        total = jnp.dot(turned, held, preferred_element_type=F32).astype(BF16)
        for i in range(2):
            out_ref[0, j + i] = total[:, i * block_b : (i + 1) * block_b]
            store = pltpu.make_async_copy(out_ref.at[0, j + i], out_hbm.at[0, j + i], sems.at[j + i])
            store.start()
            stores.append(store)
    for store in stores:
        store.wait()


def call(kernel, shapes, operands, inside=VMEM, outside=VMEM, scratch=(), dtype=BF16):
    return pl.pallas_call(
        kernel,
        out_shape=[jax.ShapeDtypeStruct(shape, dtype) for shape in shapes],
        in_specs=[inside] * len(operands),
        out_specs=[outside] * len(shapes),
        scratch_shapes=scratch,
        compiler_params=pltpu.CompilerParams(vmem_limit_bytes=32 << 20),
    )(*operands)


def body(amplitudes, factors):
    cores = lax.axis_size("core")
    chips = lax.axis_size("chip")
    cols = lax.axis_size("col")
    rows = chips * cores
    _, nj, block_a, block_b = amplitudes.shape
    block_q = factors.shape[0]
    aux = block_q * cols
    half = block_b // 2
    few = block_q // 2

    both, kept = call(
        pack_kernel,
        [(rows, 2, half + few, block_b), amplitudes.shape],
        [pltpu.with_memory_space_constraint(x, pltpu.HBM) for x in (amplitudes, factors)],
        inside=HBM,
        scratch=[pltpu.VMEM(factors.shape, BF16), pltpu.SemaphoreType.DMA((2,))],
    )
    start = ((1 - lax.axis_index("core")) * block_b).astype(jnp.uint32)
    both, start = lax.optimization_barrier((both, start))
    both = exchange(both, ROW)
    both = exchange(both.reshape(cols, half + few, block_b), "col")
    x, y = both[:, :half], both[:, half:]

    x = x.reshape(chips, 2, block_b, block_b)
    y = jnp.broadcast_to(y.reshape(1, cols * few, block_b), (chips, cols * few, block_b))
    own = exchange(jnp.concatenate([x[:, 0], y, x[:, 1]], axis=1), "chip")

    zero = jnp.uint32(0)
    other = lax.dynamic_slice(own, (zero, start, zero), (chips, block_b + aux // 2, block_b))
    other = lax.ppermute(other, "core", [(0, 1), (1, 0)])

    (early,) = call(early_kernel, [(aux // 2, block_a)], [own, kept], dtype=F32)
    (partial,) = call(fit_kernel, [(aux, block_a)], [own, other, kept, early])

    parts = exchange(partial.reshape(cols, block_q, block_a), "col")
    (copies,) = call(sum_kernel, [parts.shape], [parts])
    fitted = exchange(copies, "col").reshape(aux, block_a)

    (result,) = call(
        project_kernel,
        [amplitudes.shape],
        [fitted, own, other],
        outside=HBM,
        scratch=[pltpu.VMEM(amplitudes.shape, BF16), pltpu.SemaphoreType.DMA((nj,))],
    )
    return result


def solution(mesh):
    rows, cols = mesh.devices.shape
    fine = Mesh(mesh.devices.reshape(rows // 2, 2, cols), ("chip", "core", "col"))
    placed = (P(None, None, ROW, "col"), P("col", None, ROW))
    return jax.shard_map(
        body, mesh=fine, in_specs=placed, out_specs=P(None, None, ROW, "col"), check_vma=False
    )
```

```python
import jax
import jax.numpy as jnp
from jax import lax
from jax.experimental import pallas as pl
from jax.experimental.pallas import tpu as pltpu
from jax.sharding import Mesh, PartitionSpec as P

F32 = jnp.float32
BF16 = jnp.bfloat16
ROW = ("chip", "core")
VMEM = pl.BlockSpec(memory_space=pltpu.VMEM)
HBM = pl.BlockSpec(memory_space=pltpu.HBM)


def exchange(value, axes):
    return lax.all_to_all(value, axes, 0, 0, tiled=True)


def places(core, block_b, aux_half):
    own_t = pl.multiple_of(core * (block_b + aux_half), block_b)
    other_t = pl.multiple_of(core * aux_half, block_b)
    other_f = pl.multiple_of((1 - core) * block_b, block_b)
    return own_t, other_t, other_f


def early_kernel(own_ref, t_ref, out_ref):
    _, nj, _, block_b = t_ref.shape
    aux_half = out_ref.shape[0]
    held = jnp.concatenate([own_ref[j, pl.ds(block_b, aux_half), :] for j in range(nj)], axis=1)
    straight = jnp.concatenate([t_ref[0, j] for j in range(nj)], axis=1)
    out_ref[...] = 2.0 * lax.dot_general(
        held, straight, (((1,), (1,)), ((), ())), preferred_element_type=F32
    )


def fit_kernel(own_ref, other_ref, t_ref, early_ref, out_ref):
    _, nj, block_a, block_b = t_ref.shape
    half = block_b // 2
    aux_half = out_ref.shape[0] // 2
    core = lax.axis_index("core")
    own_t, other_t, other_f = places(core, block_b, aux_half)
    columns = []
    for side in range(2):
        blocks = []
        for j in range(nj):
            mine = own_ref[j, pl.ds(own_t + side * half, half), :]
            theirs = other_ref[j, pl.ds(other_t + side * half, half), :]
            blocks.append(jnp.where(core == 0, mine, theirs))
            blocks.append(jnp.where(core == 0, theirs, mine))
        columns.append(jnp.concatenate(blocks, axis=0))
    swapped = jnp.concatenate(columns, axis=1)
    held = jnp.concatenate([own_ref[j, pl.ds(block_b, aux_half), :] for j in range(nj)], axis=1)
    mirror = jnp.dot(held, swapped, preferred_element_type=F32)
    out_ref[pl.ds(0, aux_half), :] = (early_ref[...] - mirror).astype(BF16)
    held = jnp.concatenate([other_ref[j, pl.ds(other_f, aux_half), :] for j in range(nj)], axis=1)
    straight = jnp.concatenate([t_ref[0, j] for j in range(nj)], axis=1)
    direct = lax.dot_general(
        held, straight, (((1,), (1,)), ((), ())), preferred_element_type=F32
    )
    mirror = jnp.dot(held, swapped, preferred_element_type=F32)
    out_ref[pl.ds(aux_half, aux_half), :] = (2.0 * direct - mirror).astype(BF16)


def pack_kernel(t_hbm, f_hbm, out_ref, t_ref, f_ref, sems):
    _, nj, _, block_b = t_ref.shape
    half = block_b // 2
    few = f_ref.shape[0] // 2
    load_f = pltpu.make_async_copy(f_hbm, f_ref, sems.at[0])
    load_t = pltpu.make_async_copy(t_hbm, t_ref, sems.at[1])
    load_f.start()
    load_t.start()
    load_f.wait()
    for bit in range(2):
        for side in range(2):
            piece = f_ref[pl.ds(bit * few, few), :, pl.ds(side * block_b, block_b)]
            by_j = jnp.swapaxes(piece.astype(F32), 0, 1).astype(BF16)
            for j in range(nj):
                out_ref[2 * j + bit, side, pl.ds(half, few), :] = by_j[j]
    load_t.wait()
    for bit in range(2):
        for side in range(2):
            rows = pl.ds(side * block_b + bit * half, half)
            for j in range(nj):
                out_ref[2 * j + bit, side, pl.ds(0, half), :] = t_ref[0, j, rows, :]


def spread_kernel(both_ref, out_ref):
    chips, _, block_b = out_ref.shape
    half = block_b // 2
    count = both_ref.shape[0]
    per_chip = count // chips
    few = both_ref.shape[1] - half
    factors = both_ref[:, pl.ds(half, few), :].reshape(count * few, block_b)
    for chip in range(chips):
        out_ref[chip, pl.ds(block_b, count * few), :] = factors
        for i in range(per_chip):
            place = i * half + (i // 2) * count * few
            out_ref[chip, pl.ds(place, half), :] = both_ref[chip * per_chip + i, pl.ds(0, half), :]


def project_kernel(fitted_ref, own_ref, other_ref, out_hbm, out_ref, sems):
    _, nj, _, block_b = out_ref.shape
    aux_half = fitted_ref.shape[0] // 2
    _, _, other_f = places(lax.axis_index("core"), block_b, aux_half)
    turned = fitted_ref[...].T
    stores = []
    for j in range(0, nj, 2):
        held = jnp.concatenate(
            [
                jnp.concatenate(
                    [
                        own_ref[j + i, pl.ds(block_b, aux_half), :],
                        other_ref[j + i, pl.ds(other_f, aux_half), :],
                    ],
                    axis=0,
                )
                for i in range(2)
            ],
            axis=1,
        )
        total = jnp.dot(turned, held, preferred_element_type=F32).astype(BF16)
        for i in range(2):
            out_ref[0, j + i] = total[:, i * block_b : (i + 1) * block_b]
            store = pltpu.make_async_copy(out_ref.at[0, j + i], out_hbm.at[0, j + i], sems.at[j + i])
            store.start()
            stores.append(store)
    for store in stores:
        store.wait()


def call(kernel, shapes, operands, inside=VMEM, outside=VMEM, scratch=(), dtype=BF16):
    return pl.pallas_call(
        kernel,
        out_shape=[jax.ShapeDtypeStruct(shape, dtype) for shape in shapes],
        in_specs=[inside] * len(operands),
        out_specs=[outside] * len(shapes),
        scratch_shapes=scratch,
        compiler_params=pltpu.CompilerParams(vmem_limit_bytes=32 << 20),
    )(*operands)


def body(amplitudes, factors):
    cores = lax.axis_size("core")
    chips = lax.axis_size("chip")
    cols = lax.axis_size("col")
    rows = chips * cores
    _, nj, block_a, block_b = amplitudes.shape
    block_q = factors.shape[0]
    aux = block_q * cols
    half = block_b // 2
    few = block_q // 2

    both, kept = call(
        pack_kernel,
        [(rows, 2, half + few, block_b), amplitudes.shape],
        [pltpu.with_memory_space_constraint(x, pltpu.HBM) for x in (amplitudes, factors)],
        inside=HBM,
        scratch=[pltpu.VMEM(factors.shape, BF16), pltpu.SemaphoreType.DMA((2,))],
    )
    start = ((1 - lax.axis_index("core")) * block_b).astype(jnp.uint32)
    both, start = lax.optimization_barrier((both, start))
    both = exchange(both, ROW)
    both = exchange(both.reshape(cols, half + few, block_b), "col")

    (both,) = call(spread_kernel, [(chips, 2 * block_b + aux // 2, block_b)], [both])
    own = exchange(both, "chip")

    zero = jnp.uint32(0)
    other = lax.dynamic_slice(own, (zero, start, zero), (chips, block_b + aux // 2, block_b))
    other = lax.ppermute(other, "core", [(0, 1), (1, 0)])

    (early,) = call(early_kernel, [(aux // 2, block_a)], [own, kept], dtype=F32)
    (partial,) = call(fit_kernel, [(aux, block_a)], [own, other, kept, early])

    parts = exchange(partial.reshape(cols, block_q, block_a), "col")
    shard = jnp.sum(parts.astype(F32), axis=0).astype(BF16)
    copies = jnp.broadcast_to(shard[None], (cols, block_q, block_a))
    fitted = exchange(copies, "col").reshape(aux, block_a)

    (result,) = call(
        project_kernel,
        [amplitudes.shape],
        [fitted, own, other],
        outside=HBM,
        scratch=[pltpu.VMEM(amplitudes.shape, BF16), pltpu.SemaphoreType.DMA((nj,))],
    )
    return result


def solution(mesh):
    rows, cols = mesh.devices.shape
    fine = Mesh(mesh.devices.reshape(rows // 2, 2, cols), ("chip", "core", "col"))
    placed = (P(None, None, ROW, "col"), P("col", None, ROW))
    return jax.shard_map(
        body, mesh=fine, in_specs=placed, out_specs=P(None, None, ROW, "col"), check_vma=False
    )
```
